128 devices in a mesh: cell: 8 (over x, z_lo), rays: 16 (over y, z_hi, core).
Axes of the slice: x: 4, y: 4, z: 4 (z_hi: 2, z_lo: 2; z = z_hi * 2 + z_lo), core: 2. Of those that a mesh axis runs over, the one named last changes fastest.
Arguments:
- encodings: float32 [4096, 128, 256], P('rays', 'cell'), may hold values from -6 to 6
- spacing: float32 [4096, 128], P('rays', 'cell'), may hold values from 0.01 to 0.06
- counts: int32 [4096, 8], P('rays', 'cell'), may hold values from 1 to 16
- cell_weights: float32 [8, 4, 256, 256], P('cell'), may hold values from -0.375 to 0.375
- density_head: float32 [8, 256], P('cell'), may hold values from -0.75 to 0.75
- decoder_in: float32 [256, 256], replicated, may hold values from -0.75 to 0.75
- decoder_out: float32 [256, 3], replicated, may hold values from -0.375 to 0.375
- color_grad: float32 [4096, 3], P('rays'), may hold values from -0.75 to 0.75
Outputs:
- layer_grads: float32 [8, 4, 256, 256], P('cell')
- head_grads: float32 [8, 256], P('cell')
- decoder_in_grad: float32 [256, 256], replicated
- decoder_out_grad: float32 [256, 3], replicated
- sample_grad: float32 [4096, 128, 256], P('rays', 'cell')
The draws below stay inside these ranges and needn't reach their ends.
Inputs may be any that keep to these rules, and one draw needn't show every extreme that they name: `counts`: live samples of a ray in a cell occupy the first slots of that cell.
All inputs are finite; a program needn't handle non-finite values.
Results may differ from the reference program's by a relative error of at most 0.0003.
Values sent between devices are 32-bit elements; how exact they have to be, the bound alone decides.
A program may use at most 128 MiB of HBM per device.

```python
import math
import jax
import jax.numpy as jnp
from jax import lax

D = 256
LAYERS = 4
SLOTS = 16
COLORS = 3
CELLS = 8
RAYS = 4096
SAMPLES = 128
N_CELL = 8


def touch_ends(result, rng, least, top_value):
    dims = result.shape
    index_at = [jax.random.randint(jax.random.fold_in(rng, axis), (), 0, dims[axis]) for axis in range(len(dims))]
    result = result.at[tuple(index_at)].set(least)
    longest = dims.index(max(dims))
    index_at[longest] = (index_at[longest] + 1) % dims[longest]
    return result.at[tuple(index_at)].set(top_value)


def levels(rng, extent, pieces, smallest, largest):
    def one(position, shards_of):
        heights = jax.random.uniform(jax.random.fold_in(jax.random.fold_in(rng, 6), position), (shards_of,), jnp.float32, smallest / len(pieces), largest / len(pieces))
        return jnp.repeat(jnp.exp(heights), extent[position] // shards_of).reshape((-1,) + (1,) * (len(extent) - position - 1))

    factor_of = one(*pieces[0])
    for cut in pieces[1:]:
        factor_of = factor_of * one(*cut)
    return factor_of


def centred(key, shape, deviation, most, shards=(), kind=jnp.bfloat16):
    drawn = jax.random.normal(key, shape, jnp.float32) * deviation
    if len(shards) > 0:
        drawn = levels(key, shape, shards, -0.22, 0.18) * drawn
    return jnp.clip(drawn, min=-most, max=most).astype(kind)


def setup_inputs(seed: int = 0) -> dict:
    streams_of = jax.random.split(jax.random.key(seed), 9)
    return {
        "encodings": centred(streams_of[0], (RAYS, SAMPLES, D), 1.0, 6.0, ((0, 16), (1, 8)), jnp.float32),
        "spacing": jnp.clip(jnp.exp(math.log(0.06) - 1.7917595 * jax.random.uniform(streams_of[1], (RAYS, SAMPLES), jnp.float32) ** levels(streams_of[1], (RAYS, SAMPLES), ((0, 16), (1, 8)), -0.2, 0.2)), 0.01, 0.06),
        "counts": touch_ends(jax.random.randint(streams_of[2], (RAYS, CELLS), 1, SLOTS + 1), jax.random.fold_in(streams_of[2], 1), 1, SLOTS).astype(jnp.int32),
        "cell_weights": centred(streams_of[3], (CELLS, LAYERS, D, D), D ** -0.5, 0.375, ((0, 8),), jnp.float32),
        "density_head": centred(streams_of[4], (CELLS, D), (D // 4) ** -0.5, 0.75, ((0, 8),), jnp.float32),
        "decoder_in": centred(streams_of[5], (D, D), (D // 4) ** -0.5, 0.75, (), jnp.float32),
        "decoder_out": centred(streams_of[6], (D, COLORS), D ** -0.5, 0.375, (), jnp.float32),
        "color_grad": centred(streams_of[7], (RAYS, COLORS), 0.05, 0.75, ((0, 16),), jnp.float32),
    }


HIGH = lax.Precision.HIGHEST


def silu_slope(pre):
    sig = jax.nn.sigmoid(pre)
    return sig * (1.0 + pre * (1.0 - sig))


def network(rows, weights):
    pres = []
    hidden = rows
    for layer in range(LAYERS):
        pre = jnp.dot(hidden, weights[layer], precision=HIGH, preferred_element_type=jnp.float32)
        pres.append(pre)
        hidden = jax.nn.silu(pre)
    return hidden, pres


def cell_rows(encodings, index):
    block = encodings[:, index * SLOTS:(index + 1) * SLOTS, :]
    return block.reshape(RAYS * SLOTS, D)


def reference(encodings, spacing, counts, cell_weights, density_head, decoder_in, decoder_out, color_grad):
    slot_ids = jnp.arange(SLOTS, dtype=jnp.int32)
    live = (slot_ids[None, None, :] < counts[:, :, None]).astype(jnp.float32).reshape(RAYS, SAMPLES)
    offset = jnp.zeros((RAYS,), jnp.float32)
    pixel = jnp.zeros((RAYS, D), jnp.float32)
    z_parts, tau_parts, trans_parts, weight_parts = [], [], [], []
    for index in range(N_CELL):
        hidden, _ = network(cell_rows(encodings, index), cell_weights[index])
        z = jnp.dot(hidden, density_head[index], precision=HIGH).reshape(RAYS, SLOTS)
        sel = slice(index * SLOTS, (index + 1) * SLOTS)
        tau = live[:, sel] * jax.nn.softplus(z) * spacing[:, sel]
        depth = offset[:, None] + jnp.cumsum(tau, axis=1) - tau
        trans = jnp.exp(-depth)
        weight = trans * (-jnp.expm1(-tau))
        offset = offset + jnp.sum(tau, axis=1)
        pixel = pixel + jnp.einsum("rs,rsd->rd", weight, hidden.reshape(RAYS, SLOTS, D), precision=HIGH)
        z_parts.append(z)
        tau_parts.append(tau)
        trans_parts.append(trans)
        weight_parts.append(weight)
    pre_dec = jnp.dot(pixel, decoder_in, precision=HIGH)
    act_dec = jax.nn.silu(pre_dec)
    decoder_out_grad = jnp.dot(act_dec.T, color_grad, precision=HIGH)
    dpre = jnp.dot(color_grad, decoder_out.T, precision=HIGH) * silu_slope(pre_dec)
    decoder_in_grad = jnp.dot(pixel.T, dpre, precision=HIGH)
    pixel_grad = jnp.dot(dpre, decoder_in.T, precision=HIGH)
    c_parts = []
    for index in range(N_CELL):
        hidden, _ = network(cell_rows(encodings, index), cell_weights[index])
        c_parts.append(jnp.einsum("rsd,rd->rs", hidden.reshape(RAYS, SLOTS, D), pixel_grad, precision=HIGH))
    c_all = jnp.concatenate(c_parts, axis=1)
    weight_all = jnp.concatenate(weight_parts, axis=1)
    weighted = weight_all * c_all
    after = jnp.sum(weighted, axis=1, keepdims=True) - jnp.cumsum(weighted, axis=1)
    layer_list, head_list, sample_list = [], [], []
    for index in range(N_CELL):
        sel = slice(index * SLOTS, (index + 1) * SLOTS)
        rows = cell_rows(encodings, index)
        hidden, pres = network(rows, cell_weights[index])
        dtau = trans_parts[index] * jnp.exp(-tau_parts[index]) * c_all[:, sel] - after[:, sel]
        dz = live[:, sel] * spacing[:, sel] * jax.nn.sigmoid(z_parts[index]) * dtau
        dz_rows = dz.reshape(RAYS * SLOTS)
        head_list.append(jnp.dot(dz_rows, hidden, precision=HIGH))
        back = (weight_parts[index][:, :, None] * pixel_grad[:, None, :]).reshape(RAYS * SLOTS, D)
        back = back + dz_rows[:, None] * density_head[index][None, :]
        grads = [None] * LAYERS
        for layer in reversed(range(LAYERS)):
            dp = back * silu_slope(pres[layer])
            source = rows if layer == 0 else jax.nn.silu(pres[layer - 1])
            grads[layer] = jnp.dot(source.T, dp, precision=HIGH)
            back = jnp.dot(dp, cell_weights[index, layer].T, precision=HIGH)
        layer_list.append(jnp.stack(grads))
        sample_list.append(back.reshape(RAYS, SLOTS, D))
    return (jnp.stack(layer_list), jnp.stack(head_list), decoder_in_grad, decoder_out_grad,
            jnp.concatenate(sample_list, axis=1))
```

```python
import functools

import jax
import jax.numpy as jnp
from jax import lax
from jax.experimental import pallas as pl
from jax.experimental.pallas import tpu as pltpu
from jax.sharding import PartitionSpec as P

F32, BF16 = jnp.float32, jnp.bfloat16
D, LAYERS, SLOTS, COLORS = 256, 4, 16, 3
GROUP = 128
NT = (((1,), (1,)), ((), ()))
NN = (((1,), (0,)), ((), ()))
TN = (((0,), (0,)), ((), ()))


def mm(a, b, dims):
    return lax.dot_general(a, b, dims, preferred_element_type=F32)


def split(v):
    hi = v.astype(BF16)
    return hi, (v - hi.astype(F32)).astype(BF16)


def left3(hi, lo, axis):
    return jnp.concatenate([hi, hi, lo], axis=axis)


def right3(hi, lo, axis):
    return jnp.concatenate([hi, lo, hi], axis=axis)


def silu_and_slope(pre):
    sig = jax.nn.sigmoid(pre)
    act = pre * sig
    return act, sig + act * (1.0 - sig)


def softplus(z):
    y = jnp.exp(-jnp.abs(z))
    s = y / (2.0 + y)
    q = s * s
    series = 1.0 / 17.0
    for odd in (15, 13, 11, 9, 7, 5, 3, 1):
        series = series * q + 1.0 / odd
    return jnp.maximum(z, 0.0) + 2.0 * s * series


def one_minus_exp(tau):
    series = 1.0
    for k in (7, 6, 5, 4, 3, 2):
        series = 1.0 - tau * series * (1.0 / k)
    return jnp.where(tau < 0.25, tau * series, 1.0 - jnp.exp(-tau))


def cumulative(v):
    rows = lax.broadcasted_iota(jnp.int32, v.shape, 0)
    for step in (1, 2, 4, 8):
        v = v + jnp.where(rows >= step, pltpu.roll(v, step, 0), 0.0)
    return v


def kernel(
    n_cell, x_hbm, sp_ref, cnt_ref, w_ref, head_ref, din_ref, dout_ref, cg_ref,
    lg_ref, hg_ref, ig_ref, og_ref, sg_hbm,
    x_ref, h_ref, s_ref, f_ref, dph_ref, dpl_ref,
    wt_ref, wb_ref, v_ref, dv_ref, dh_ref, headt_ref, dot_ref, pad_ref,
    z_ref, sm_ref, et_ref, hacc_ref,
    p_ref, pr_ref, t_ref, tr_ref, q_ref, qs_ref, px_ref, dpre_ref, ogs_ref,
    igs_ref, igr_ref, ex_ref, exc_ref, eb_ref, ef_ref, igf_ref,
    g_ref, cr_ref, half_ref, rr_ref, red_ref,
    x_sem, o_sem, e1_send, e1_recv, t_send, t_recv, e2_send, e2_recv,
    ig_send, ig_recv, ec_send, ec_recv, eb_send, eb_recv, ef_send, ef_recv, ia_send, ia_recv,
    c_send, c_recv, r_send, r_recv, a_send, a_recv, s_send, s_recv,
):
    me = lax.axis_index("cell")
    ray = lax.axis_index("rays")
    core = lax.rem(ray, 2)
    spot = ray // 2
    sibling = ray + 1 - 2 * core
    n_groups = sp_ref.shape[0] // GROUP
    n_spot = 8
    owned = GROUP // n_cell
    wide = 8 * GROUP
    my_rows = pl.ds(pl.multiple_of(me * owned, 8), owned)

    def take(g, side):
        part = pl.ds(g * GROUP * SLOTS, GROUP * SLOTS)
        lanes = pl.ds(side * 128, 128)
        return pltpu.make_async_copy(x_hbm.at[part, lanes], x_ref.at[side, part, :], x_sem.at[g, side])

    def give(g, side):
        part = pl.ds(g * GROUP * SLOTS, GROUP * SLOTS)
        lanes = pl.ds(side * 128, 128)
        return pltpu.make_async_copy(x_ref.at[side, part, :], sg_hbm.at[part, lanes], o_sem.at[g, side])

    for g in range(n_groups):
        for side in range(2):
            take(g, side).start()

    def cell_peer(d):
        return {"cell": lax.rem(me + d, n_cell)}

    def spot_peer(d):
        return {"rays": 2 * lax.rem(spot + d, n_spot) + core}

    barrier = pltpu.get_barrier_semaphore()

    def greet(d, _):
        pl.semaphore_signal(barrier, inc=1, device_id=cell_peer(d))
        pl.semaphore_signal(barrier, inc=1, device_id=spot_peer(d))
        return 0

    lax.fori_loop(1, n_cell, greet, 0)
    pl.semaphore_signal(barrier, inc=1, device_id={"rays": sibling})

    def remote(src, dst, send, recv, device):
        return pltpu.make_async_remote_copy(
            src_ref=src, dst_ref=dst, send_sem=send, recv_sem=recv, device_id=device
        )

    def each(count, make, act):
        def body(d, _):
            act(make(d))
            return 0

        lax.fori_loop(1, count, body, 0)

    def e1(g, d):
        to = lax.rem(me + d, n_cell)
        rows = pl.ds(pl.multiple_of(to * owned, 8), owned)
        return remote(p_ref.at[g, rows, :], pr_ref.at[g, me], e1_send.at[g, d], e1_recv.at[g, d], cell_peer(d))

    def t1(g, d):
        return remote(t_ref.at[g], tr_ref.at[g, me], t_send.at[g, d], t_recv.at[g, d], cell_peer(d))

    def e2(g, d):
        return remote(qs_ref.at[g], q_ref.at[g, my_rows, :], e2_send.at[g, d], e2_recv.at[g, d], cell_peer(d))

    def igc(d):
        to = lax.rem(me + d, n_cell)
        return remote(igs_ref.at[to], igr_ref.at[me], ig_send.at[d], ig_recv.at[d], cell_peer(d))

    ex_mine = pl.ds(pl.multiple_of(core * 24, 8), 24)
    ex_other = pl.ds(pl.multiple_of((1 - core) * 24, 8), 24)

    def ecc():
        return remote(ex_ref.at[ex_other, :], exc_ref, ec_send.at[0], ec_recv.at[0], {"rays": sibling})

    def ebc(d):
        return remote(eb_ref.at[spot], eb_ref.at[spot], eb_send.at[d], eb_recv.at[d], spot_peer(d))

    def efc():
        return remote(ef_ref.at[ex_mine, :], ef_ref.at[ex_mine, :], ef_send.at[0], ef_recv.at[0], {"rays": sibling})

    def iac(d):
        return remote(ef_ref.at[pl.ds(0, 32), :], igf_ref.at[me], ia_send.at[d], ia_recv.at[d], cell_peer(d))

    def cc(l):
        other = pl.ds(pl.multiple_of((1 - core) * 128, 128), 128)
        return remote(g_ref.at[l, other, :], cr_ref.at[l], c_send.at[l], c_recv.at[l], {"rays": sibling})

    def rc(l, d):
        to = lax.rem(spot + d, n_spot)
        rows = pl.ds(pl.multiple_of(to * 16, 16), 16)
        return remote(half_ref.at[l, rows, :], rr_ref.at[l, spot], r_send.at[l, d], r_recv.at[l, d], spot_peer(d))

    red_half = pl.ds(pl.multiple_of(core * 128, 128), 128)
    red_block = pl.ds(pl.multiple_of(core * 128 + spot * 16, 16), 16)

    def ac(l, d):
        return remote(red_ref.at[l, red_block, :], red_ref.at[l, red_block, :], a_send.at[l, d], a_recv.at[l, d], spot_peer(d))

    def sc(l):
        return remote(red_ref.at[l, red_half, :], red_ref.at[l, red_half, :], s_send.at[l], s_recv.at[l], {"rays": sibling})

    start = lambda c: c.start()
    arrived = lambda c: c.wait_recv()
    sent = lambda c: c.wait_send()

    for l in range(LAYERS):
        hi, lo = split(w_ref[l])
        wb_ref[l] = left3(hi, lo, 1)
        thi, tlo = split(w_ref[l].T)
        wt_ref[l] = left3(thi, tlo, 1)
        if l == 0:
            v_ref[...] = left3(thi, tlo, 0)
    headt_ref[...] = jnp.broadcast_to(head_ref[...], (GROUP, D)).T
    for g in range(n_groups):
        rays = pl.ds(g * GROUP, GROUP)
        pad_ref[...] = jnp.zeros_like(pad_ref)
        pad_ref[:, 0:SLOTS] = sp_ref[rays, :]
        spacing = pad_ref[...].T[0:SLOTS, :]
        count = jnp.broadcast_to(cnt_ref[rays, :].astype(F32), (GROUP, GROUP)).T[0:SLOTS, :]
        slot = lax.broadcasted_iota(jnp.int32, (SLOTS, GROUP), 0).astype(F32)
        sm_ref[g, 0] = jnp.where(slot < count, spacing, 0.0)

    def x_rows(g, s):
        return pl.ds(g * GROUP * SLOTS + s, GROUP, stride=SLOTS)

    def x_load(g, s):
        return jnp.concatenate([x_ref[side, x_rows(g, s), :] for side in range(2)], axis=1)

    def forward(g, half):
        chunk = 2 * g + half
        hidden = [None] * 4
        for q in range(4):
            slabs = [x_load(g, 8 * half + 2 * q + t) for t in range(2)]
            hidden[q] = right3(*split(jnp.concatenate(slabs, axis=0)), 1)
        for l in range(LAYERS):
            for q in range(4):
                columns = pl.ds(q * 2 * GROUP, 2 * GROUP)
                pre = mm(wt_ref[l], hidden[q], NT if l == 0 else NN)
                act, slope = silu_and_slope(pre)
                s_ref[l, chunk, :, columns] = slope
                if l < LAYERS - 1:
                    hi, lo = split(act)
                    h_ref[l, 0, chunk, :, columns] = hi
                    h_ref[l, 1, chunk, :, columns] = lo
                    hidden[q] = right3(hi, lo, 0)
                else:
                    f_ref[chunk, :, columns] = act
                    for t in range(2):
                        z = jnp.sum(act[:, t * GROUP:(t + 1) * GROUP] * headt_ref[...], axis=0, keepdims=True)
                        z_ref[g, pl.ds(8 * half + 2 * q + t, 1), :] = z

    def slot_of(ref, g, s):
        return ref[2 * g + s // 8, :, (s % 8) * GROUP:(s % 8 + 1) * GROUP]

    def rays_forward(g):
        z = z_ref[g]
        tau = softplus(z) * sm_ref[g, 0]
        incl = cumulative(tau)
        excl = incl - tau
        opaque = one_minus_exp(tau)
        sm_ref[g, 1] = tau
        sm_ref[g, 2] = excl
        sm_ref[g, 3] = opaque
        sm_ref[g, 4] = sm_ref[g, 0] * jax.nn.sigmoid(z)
        total = jnp.broadcast_to(incl[SLOTS - 1:SLOTS, :], (8, GROUP))
        t_ref[g] = total
        tr_ref[g, me] = total
        each(n_cell, functools.partial(t1, g), start)
        local = jnp.exp(-excl) * opaque
        acc = slot_of(f_ref, g, 0) * local[0:1, :]
        for s in range(1, SLOTS):
            acc = acc + slot_of(f_ref, g, s) * local[s:s + 1, :]
        p_ref[g] = acc.T
        each(n_cell, functools.partial(e1, g), start)
        pr_ref[g, me] = p_ref[g, my_rows, :]

    def decode(g):
        each(n_cell, functools.partial(t1, g), arrived)
        each(n_cell, functools.partial(e1, g), arrived)
        offset = jnp.zeros((1, GROUP), F32)
        own = jnp.zeros((1, GROUP), F32)
        rows = []
        for j in range(n_cell):
            rows.append(jnp.exp(-offset))
            own = jnp.where(me == j, offset, own)
            offset = offset + tr_ref[g, j][0:1, :]
        sm_ref[g, 5] = jnp.broadcast_to(own, (SLOTS, GROUP))
        et_ref[...] = jnp.concatenate(rows + [jnp.zeros((GROUP - n_cell, GROUP), F32)], axis=0).T
        et = et_ref[my_rows, :]
        parts = [pr_ref[g, j] * et[:, j:j + 1] for j in range(n_cell)]
        pixel = parts[0]
        for j in range(1, n_cell):
            pixel = pixel + parts[j]
        px_ref[g] = pixel
        pre = mm(right3(*split(pixel), 1), dv_ref[...], NN)
        colors = cg_ref[pl.ds(pl.multiple_of(g * GROUP + me * owned, 8), owned), :]
        act, slope = silu_and_slope(pre)
        reach = colors[:, 0:1] * dot_ref[0:1, :]
        for c in range(1, COLORS):
            reach = reach + colors[:, c:c + 1] * dot_ref[c:c + 1, :]
        dpre = reach * slope
        dpre_ref[g] = dpre
        for c in range(COLORS):
            ogs_ref[g, c:c + 1, :] = jnp.sum(act * colors[:, c:c + 1], axis=0, keepdims=True)
        grad = mm(right3(*split(dpre), 1), dh_ref[...], NT)
        lanes = lax.broadcasted_iota(jnp.int32, (owned, GROUP), 1)
        later = jnp.zeros((owned, GROUP), F32)
        for j in range(1, n_cell):
            value = jnp.sum(parts[j] * grad, axis=1, keepdims=True)
            later = later + jnp.where(lanes < j, value, 0.0)
        payload = jnp.concatenate([grad, later], axis=1)
        qs_ref[g] = payload
        each(n_cell, functools.partial(e2, g), start)
        q_ref[g, my_rows, :] = payload

    def decoder_grads():
        px = right3(*split(px_ref[...].reshape(n_groups * owned, D)), 0)
        dp = left3(*split(dpre_ref[...].reshape(n_groups * owned, D)), 0)
        grad = mm(px, dp, TN)
        colors = ogs_ref[0]
        for g in range(1, n_groups):
            colors = colors + ogs_ref[g]
        for j in range(n_cell):
            igs_ref[j, 0:32, :] = grad[32 * j:32 * j + 32, :]
            igs_ref[j, 32:40, :] = colors
        each(n_cell, igc, start)
        igr_ref[me] = igs_ref[me]

    def rays_backward(g):
        each(n_cell, functools.partial(e2, g), arrived)
        gradt = q_ref[g, :, 0:D].T
        latert = q_ref[g, :, D:D + GROUP].T[0:8, :]
        picked = lax.broadcasted_iota(jnp.int32, (8, GROUP), 0) == me
        later = jnp.sum(jnp.where(picked, latert, 0.0), axis=0, keepdims=True)
        et_ref[...] = jnp.zeros_like(et_ref)
        for s in range(SLOTS):
            et_ref[s:s + 1, :] = jnp.sum(slot_of(f_ref, g, s) * gradt, axis=0, keepdims=True)
        c = et_ref[0:SLOTS, :]
        tau = sm_ref[g, 1]
        trans = jnp.exp(-(sm_ref[g, 5] + sm_ref[g, 2]))
        weight = trans * sm_ref[g, 3]
        incl = cumulative(weight * c)
        after = later + incl[SLOTS - 1:SLOTS, :] - incl
        dz = sm_ref[g, 4] * (trans * jnp.exp(-tau) * c - after)
        sm_ref[g, 6] = weight
        sm_ref[g, 7] = dz
        q_ref[g, :, 0:GROUP] = gradt[0:GROUP, :]
        q_ref[g, :, GROUP:2 * GROUP] = gradt[GROUP:D, :]

    def head_step(chunk, l):
        g, half = chunk // 2, lax.rem(chunk, 2)
        for q in range(8):
            row = pl.ds(8 * half + q, 1)
            weight, dz = sm_ref[g, 6, row, :], sm_ref[g, 7, row, :]
            columns = pl.ds(q * GROUP, GROUP)
            for part in range(2):
                rows = pl.ds(part * 128, 128)
                back = q_ref[g, :, part * GROUP:(part + 1) * GROUP] * weight + headt_ref[rows, :] * dz
                hacc_ref[rows, :] += f_ref[chunk, rows, columns] * dz
                hi, lo = split(back * s_ref[LAYERS - 1, chunk, rows, columns])
                dph_ref[chunk, rows, columns] = hi
                dpl_ref[chunk, rows, columns] = lo

    def layer_step(chunk, l):
        hi, lo = dph_ref[chunk], dpl_ref[chunk]
        source = right3(h_ref[l - 1, 0, chunk], h_ref[l - 1, 1, chunk], 1)
        g_ref[l] += mm(source, left3(hi, lo, 1), NT)
        for q in range(4):
            columns = slice(q * 2 * GROUP, (q + 1) * 2 * GROUP)
            back = mm(wb_ref[l], right3(hi[:, columns], lo[:, columns], 0), NN)
            nhi, nlo = split(back * s_ref[l - 1, chunk, :, columns])
            dph_ref[chunk, :, columns] = nhi
            dpl_ref[chunk, :, columns] = nlo

    def first_grad(chunk):
        g, half = chunk // 2, lax.rem(chunk, 2)
        rows = jnp.concatenate([x_load(g, 8 * half + q) for q in range(8)], axis=0)
        g_ref[0] += mm(left3(dph_ref[chunk], dpl_ref[chunk], 1), right3(*split(rows), 0), NN)

    def first_back(chunk):
        g, half = chunk // 2, lax.rem(chunk, 2)
        for q in range(4):
            columns = slice(q * 2 * GROUP, (q + 1) * 2 * GROUP)
            back = mm(right3(dph_ref[chunk, :, columns], dpl_ref[chunk, :, columns], 0), v_ref[...], TN)
            for t in range(2):
                for side in range(2):
                    x_ref[side, x_rows(g, 8 * half + 2 * q + t), :] = back[
                        t * GROUP:(t + 1) * GROUP, side * 128:(side + 1) * 128
                    ]

    def sum_a(l):
        cc(l).start()

    def sum_b(l):
        cc(l).wait_recv()
        half_ref[l] = g_ref[l, red_half, :] + cr_ref[l]
        each(n_spot, functools.partial(rc, l), start)
        rr_ref[l, spot] = half_ref[l, pl.ds(pl.multiple_of(spot * 16, 16), 16), :]

    def sum_c(l):
        each(n_spot, functools.partial(rc, l), arrived)
        total = rr_ref[l, 0]
        for j in range(1, n_spot):
            total = total + rr_ref[l, j]
        red_ref[l, red_block, :] = total
        each(n_spot, functools.partial(ac, l), start)

    def sum_d(l):
        each(n_spot, functools.partial(ac, l), arrived)
        sc(l).start()

    def sum_e(l):
        sc(l).wait_recv()
        lg_ref[l] = red_ref[l]

    def extra_a():
        each(n_cell, igc, arrived)
        total = igr_ref[0]
        for j in range(1, n_cell):
            total = total + igr_ref[j]
        ex_ref[0:40, :] = total
        ex_ref[40:48, :] = jnp.broadcast_to(jnp.sum(hacc_ref[...].T, axis=0, keepdims=True), (8, D))
        ecc().start()

    def extra_b():
        ecc().wait_recv()
        eb_ref[spot] = ex_ref[ex_mine, :] + exc_ref[...]
        each(n_spot, ebc, start)

    def extra_c():
        each(n_spot, ebc, arrived)
        total = eb_ref[0]
        for j in range(1, n_spot):
            total = total + eb_ref[j]
        ef_ref[ex_mine, :] = total
        efc().start()

    def extra_d():
        efc().wait_recv()
        each(n_cell, iac, start)
        igf_ref[me] = ef_ref[0:32, :]

    def extra_e():
        each(n_cell, iac, arrived)
        ig_ref[...] = igf_ref[...].reshape(D, D)
        pad_ref[...] = jnp.zeros_like(pad_ref)
        for part in range(2):
            pad_ref[0:8, :] = ef_ref[32:40, part * 128:(part + 1) * 128]
            og_ref[part * 128:(part + 1) * 128, :] = pad_ref[...].T[:, 0:COLORS]
        hg_ref[...] = ef_ref[40:41, :]

    def wait_x(g):
        for side in range(2):
            take(g, side).wait()

    def forward_loop(g):
        def body(half, _):
            forward(g, half)
            return 0

        lax.fori_loop(0, 2, body, 0)

    wait_x(0)
    forward_loop(0)
    pl.semaphore_wait(barrier, 2 * (n_cell - 1) + 1)
    rays_forward(0)
    hi, lo = split(din_ref[...])
    dv_ref[...] = left3(hi, lo, 0)
    dh_ref[...] = left3(hi, lo, 1)
    for part in range(2):
        pad_ref[...] = jnp.zeros_like(pad_ref)
        pad_ref[:, 0:COLORS] = dout_ref[part * 128:(part + 1) * 128, :]
        dot_ref[:, part * 128:(part + 1) * 128] = pad_ref[...].T[0:8, :]
    ogs_ref[...] = jnp.zeros_like(ogs_ref)
    g_ref[...] = jnp.zeros_like(g_ref)
    hacc_ref[...] = jnp.zeros_like(hacc_ref)
    wait_x(1)
    forward_loop(1)
    decode(0)
    rays_forward(1)
    rays_backward(0)

    def top(chunk, _):
        head_step(chunk, LAYERS - 1)
        layer_step(chunk, LAYERS - 1)
        return 0

    lax.fori_loop(0, 2, top, 0)
    decode(1)
    decoder_grads()
    rays_backward(1)
    lax.fori_loop(2, 4, top, 0)
    sum_a(3)
    extra_a()

    def middle(l):
        def body(chunk, _):
            layer_step(chunk, l)
            return 0

        return body

    lax.fori_loop(0, 2, middle(2), 0)
    sum_b(3)
    extra_b()
    lax.fori_loop(2, 4, middle(2), 0)
    sum_a(2)
    sum_c(3)
    extra_c()
    lax.fori_loop(0, 2, middle(1), 0)
    sum_b(2)
    sum_d(3)
    extra_d()
    lax.fori_loop(2, 4, middle(1), 0)
    sum_a(1)
    sum_c(2)
    sum_e(3)

    def first(chunk, _):
        first_grad(chunk)
        return 0

    lax.fori_loop(0, 2, first, 0)
    sum_b(1)
    sum_d(2)
    lax.fori_loop(2, 4, first, 0)
    g_ref[0] = g_ref[0].T
    sum_a(0)
    sum_c(1)
    sum_e(2)

    def last(chunk, _):
        first_back(chunk)
        return 0

    lax.fori_loop(0, 2, last, 0)
    for side in range(2):
        give(0, side).start()
    sum_b(0)
    sum_d(1)
    lax.fori_loop(2, 4, last, 0)
    for side in range(2):
        give(1, side).start()
    sum_c(0)
    sum_e(1)
    extra_e()
    sum_d(0)
    sum_e(0)
    for g in range(n_groups):
        for side in range(2):
            give(g, side).wait()
    for g in range(n_groups):
        each(n_cell, functools.partial(t1, g), sent)
        each(n_cell, functools.partial(e1, g), sent)
        each(n_cell, functools.partial(e2, g), sent)
    each(n_cell, igc, sent)
    ecc().wait_send()
    each(n_spot, ebc, sent)
    efc().wait_send()
    each(n_cell, iac, sent)
    for l in range(LAYERS):
        cc(l).wait_send()
        each(n_spot, functools.partial(rc, l), sent)
        each(n_spot, functools.partial(ac, l), sent)
        sc(l).wait_send()


def local(n_cell, encodings, spacing, counts, cell_weights, density_head, decoder_in, decoder_out, color_grad):
    rays, slots, width = encodings.shape
    rows = rays * slots
    groups, chunks, wide = rays // GROUP, rows // (8 * GROUP), 8 * GROUP
    owned = GROUP // n_cell
    vmem = pl.BlockSpec(memory_space=pltpu.VMEM)
    anywhere = pl.BlockSpec(memory_space=pl.ANY)
    dma = pltpu.SemaphoreType.DMA
    V = pltpu.VMEM
    scratch = [
        V((2, rows, 128), F32),
        V((LAYERS - 1, 2, chunks, D, wide), BF16),
        V((LAYERS, chunks, D, wide), F32),
        V((chunks, D, wide), F32),
        V((chunks, D, wide), BF16),
        V((chunks, D, wide), BF16),
        V((LAYERS, D, 3 * D), BF16),
        V((LAYERS, D, 3 * D), BF16),
        V((3 * D, D), BF16),
        V((3 * D, D), BF16),
        V((D, 3 * D), BF16),
        V((D, GROUP), F32),
        V((8, D), F32),
        V((GROUP, GROUP), F32),
        V((groups, SLOTS, GROUP), F32),
        V((groups, 8, SLOTS, GROUP), F32),
        V((GROUP, GROUP), F32),
        V((D, GROUP), F32),
        V((groups, GROUP, D), F32),
        V((groups, n_cell, owned, D), F32),
        V((groups, 8, GROUP), F32),
        V((groups, n_cell, 8, GROUP), F32),
        V((groups, GROUP, D + GROUP), F32),
        V((groups, owned, D + GROUP), F32),
        V((groups, owned, D), F32),
        V((groups, owned, D), F32),
        V((groups, 8, D), F32),
        V((n_cell, 40, D), F32),
        V((n_cell, 40, D), F32),
        V((48, D), F32),
        V((24, D), F32),
        V((8, 24, D), F32),
        V((48, D), F32),
        V((n_cell, 32, D), F32),
        V((LAYERS, D, D), F32),
        V((LAYERS, 128, D), F32),
        V((LAYERS, 128, D), F32),
        V((LAYERS, 8, 16, D), F32),
        V((LAYERS, D, D), F32),
        dma((groups, 2)), dma((groups, 2)),
        dma((groups, n_cell)), dma((groups, n_cell)),
        dma((groups, n_cell)), dma((groups, n_cell)),
        dma((groups, n_cell)), dma((groups, n_cell)),
        dma((n_cell,)), dma((n_cell,)),
        dma((1,)), dma((1,)),
        dma((8,)), dma((8,)),
        dma((1,)), dma((1,)),
        dma((n_cell,)), dma((n_cell,)),
        dma((LAYERS,)), dma((LAYERS,)),
        dma((LAYERS, 8)), dma((LAYERS, 8)),
        dma((LAYERS, 8)), dma((LAYERS, 8)),
        dma((LAYERS,)), dma((LAYERS,)),
    ]
    layer, head, din, dout, sample = pl.pallas_call(
        functools.partial(kernel, n_cell),
        out_shape=[
            jax.ShapeDtypeStruct((LAYERS, D, D), F32),
            jax.ShapeDtypeStruct((1, D), F32),
            jax.ShapeDtypeStruct((D, D), F32),
            jax.ShapeDtypeStruct((D, COLORS), F32),
            jax.ShapeDtypeStruct((rows, D), F32),
        ],
        in_specs=[anywhere] + [vmem] * 7,
        out_specs=[vmem] * 4 + [anywhere],
        scratch_shapes=scratch,
        compiler_params=pltpu.CompilerParams(
            collective_id=0, has_side_effects=True, vmem_limit_bytes=62 << 20
        ),
    )(
        encodings.reshape(rows, width), spacing, counts, cell_weights[0], density_head,
        decoder_in, decoder_out, color_grad,
    )
    return layer[None], head, din, dout, sample.reshape(rays, slots, width)


def solution(mesh):
    return jax.shard_map(
        functools.partial(local, mesh.shape["cell"]),
        mesh=mesh,
        in_specs=(
            P("rays", "cell", None), P("rays", "cell"), P("rays", "cell"), P("cell", None, None, None),
            P("cell", None), P(None, None), P(None, None), P("rays", None),
        ),
        out_specs=(
            P("cell", None, None, None), P("cell", None), P(None, None), P(None, None), P("rays", "cell", None),
        ),
        check_vma=False,
    )
```

```python
import functools

import jax
import jax.numpy as jnp
from jax import lax
from jax.experimental import pallas as pl
from jax.experimental.pallas import tpu as pltpu
from jax.sharding import PartitionSpec as P

F32, BF16 = jnp.float32, jnp.bfloat16
D, LAYERS, SLOTS, COLORS = 256, 4, 16, 3
GROUP = 128
NT = (((1,), (1,)), ((), ()))
NN = (((1,), (0,)), ((), ()))
TN = (((0,), (0,)), ((), ()))


def mm(a, b, dims):
    return lax.dot_general(a, b, dims, preferred_element_type=F32)


def split(v):
    hi = v.astype(BF16)
    return hi, (v - hi.astype(F32)).astype(BF16)


def left3(hi, lo, axis):
    return jnp.concatenate([hi, hi, lo], axis=axis)


def right3(hi, lo, axis):
    return jnp.concatenate([hi, lo, hi], axis=axis)


def silu_and_slope(pre):
    sig = jax.nn.sigmoid(pre)
    act = pre * sig
    return act, sig + act * (1.0 - sig)


def softplus(z):
    y = jnp.exp(-jnp.abs(z))
    s = y / (2.0 + y)
    q = s * s
    series = 1.0 / 17.0
    for odd in (15, 13, 11, 9, 7, 5, 3, 1):
        series = series * q + 1.0 / odd
    return jnp.maximum(z, 0.0) + 2.0 * s * series


def one_minus_exp(tau):
    series = 1.0
    for k in (7, 6, 5, 4, 3, 2):
        series = 1.0 - tau * series * (1.0 / k)
    return jnp.where(tau < 0.25, tau * series, 1.0 - jnp.exp(-tau))


def cumulative(v):
    rows = lax.broadcasted_iota(jnp.int32, v.shape, 0)
    for step in (1, 2, 4, 8):
        v = v + jnp.where(rows >= step, pltpu.roll(v, step, 0), 0.0)
    return v


def kernel(
    n_cell, x_hbm, sp_hbm, cnt_hbm, w_hbm, head_hbm, din_hbm, dout_hbm, cg_hbm,
    red_ref, hg_ref, igf_ref, og_ref, x_ref,
    sp_ref, cnt_ref, w_ref, head_ref, din_ref, dout_ref, cg_ref, cgt_ref,
    h_ref, s_ref, f_ref, dph_ref, dpl_ref,
    wt_ref, wb_ref, v_ref, dv_ref, dh_ref, headt_ref,
    z_ref, sm_ref, et_ref, hacc_ref,
    p_ref, pr_ref, t_ref, tr_ref, q_ref, qs_ref, px_ref, dpre_ref, ogs_ref,
    igs_ref, igr_ref, ex_ref, exc_ref, eb_ref, ef_ref,
    g_ref, cr_ref, half_ref, rr_ref,
    x_sem, in_sem, e1_send, e1_recv, t_send, t_recv, e2_send, e2_recv,
    ig_send, ig_recv, ec_send, ec_recv, eb_send, eb_recv, ef_send, ef_recv, ia_send, ia_recv,
    c_send, c_recv, r_send, r_recv, a_send, a_recv, s_send, s_recv,
):
    me = lax.axis_index("cell")
    ray = lax.axis_index("rays")
    core = lax.rem(ray, 2)
    spot = ray // 2
    sibling = ray + 1 - 2 * core
    n_groups = sp_ref.shape[1] // GROUP
    n_spot = 8
    owned = GROUP // n_cell
    wide = 8 * GROUP
    my_rows = pl.ds(pl.multiple_of(me * owned, 8), owned)

    def take(g, side):
        part = pl.ds(g * GROUP * SLOTS, GROUP * SLOTS)
        lanes = pl.ds(side * 128, 128)
        return pltpu.make_async_copy(x_hbm.at[part, lanes], x_ref.at[side, part, :], x_sem.at[g, side])

    pairs = (
        (head_hbm, head_ref), (sp_hbm, sp_ref), (cnt_hbm, cnt_ref), (cg_hbm, cg_ref), (dout_hbm, dout_ref),
        (din_hbm, din_ref),
    )
    small = [pltpu.make_async_copy(src, dst, in_sem.at[n]) for n, (src, dst) in enumerate(pairs)]
    weights = [
        pltpu.make_async_copy(w_hbm.at[l], w_ref.at[l], in_sem.at[len(pairs) + l]) for l in range(LAYERS)
    ]
    weights[0].start()
    for g in range(n_groups):
        for side in range(2):
            take(g, side).start()
        if g == 0:
            for c in weights[1:] + small:
                c.start()

    def cell_peer(d):
        return {"cell": lax.rem(me + d, n_cell)}

    def spot_peer(d):
        return {"rays": 2 * lax.rem(spot + d, n_spot) + core}

    barrier = pltpu.get_barrier_semaphore()

    def greet(d, _):
        pl.semaphore_signal(barrier, inc=1, device_id=cell_peer(d))
        pl.semaphore_signal(barrier, inc=1, device_id=spot_peer(d))
        return 0

    lax.fori_loop(1, n_cell, greet, 0)
    pl.semaphore_signal(barrier, inc=1, device_id={"rays": sibling})

    def remote(src, dst, send, recv, device):
        return pltpu.make_async_remote_copy(
            src_ref=src, dst_ref=dst, send_sem=send, recv_sem=recv, device_id=device
        )

    def each(count, make):
        def body(d, _):
            make(d).start()
            return 0

        lax.fori_loop(1, count, body, 0)

    def e1(g, d):
        to = lax.rem(me + d, n_cell)
        rows = pl.ds(pl.multiple_of(to * owned, 8), owned)
        return remote(p_ref.at[g, rows, :], pr_ref.at[g, me], e1_send.at[g], e1_recv.at[g], cell_peer(d))

    def e1_all(g):
        blocks = pr_ref.at[g, pl.ds(0, n_cell - 1)]
        return remote(blocks, blocks, e1_send.at[g], e1_recv.at[g], cell_peer(1))

    def t1(g, d):
        return remote(t_ref.at[g], tr_ref.at[g, me], t_send.at[g], t_recv.at[g], cell_peer(d))

    def t1_all(g):
        blocks = tr_ref.at[g, pl.ds(0, n_cell - 1)]
        return remote(blocks, blocks, t_send.at[g], t_recv.at[g], cell_peer(1))

    def e2(g, d):
        return remote(qs_ref.at[g], q_ref.at[g, my_rows, :], e2_send.at[g], e2_recv.at[g], cell_peer(d))

    def e2_all(g):
        blocks = q_ref.at[g, pl.ds(0, GROUP - owned), :]
        return remote(blocks, blocks, e2_send.at[g], e2_recv.at[g], cell_peer(1))

    def igc(d):
        to = lax.rem(me + d, n_cell)
        return remote(igs_ref.at[to], igr_ref.at[me], ig_send.at[0], ig_recv.at[0], cell_peer(d))

    def igc_all():
        blocks = igr_ref.at[pl.ds(0, n_cell - 1)]
        return remote(blocks, blocks, ig_send.at[0], ig_recv.at[0], cell_peer(1))

    ex_mine = pl.ds(pl.multiple_of(core * 24, 8), 24)
    ex_other = pl.ds(pl.multiple_of((1 - core) * 24, 8), 24)

    def ecc():
        return remote(ex_ref.at[ex_other, :], exc_ref, ec_send.at[0], ec_recv.at[0], {"rays": sibling})

    def ebc(d):
        return remote(eb_ref.at[spot], eb_ref.at[spot], eb_send.at[0], eb_recv.at[0], spot_peer(d))

    def ebc_all():
        blocks = eb_ref.at[pl.ds(0, n_spot - 1)]
        return remote(blocks, blocks, eb_send.at[0], eb_recv.at[0], spot_peer(1))

    def efc():
        return remote(ef_ref.at[ex_mine, :], ef_ref.at[ex_mine, :], ef_send.at[0], ef_recv.at[0], {"rays": sibling})

    def iac(d):
        return remote(ef_ref.at[pl.ds(0, 32), :], igf_ref.at[me], ia_send.at[0], ia_recv.at[0], cell_peer(d))

    def iac_all():
        blocks = igf_ref.at[pl.ds(0, n_cell - 1)]
        return remote(blocks, blocks, ia_send.at[0], ia_recv.at[0], cell_peer(1))

    def cc(l):
        other = pl.ds(pl.multiple_of((1 - core) * 128, 128), 128)
        return remote(g_ref.at[l, other, :], cr_ref.at[l], c_send.at[l], c_recv.at[l], {"rays": sibling})

    def rc(l, d):
        to = lax.rem(spot + d, n_spot)
        rows = pl.ds(pl.multiple_of(to * 16, 16), 16)
        return remote(half_ref.at[l, rows, :], rr_ref.at[l, spot], r_send.at[l], r_recv.at[l], spot_peer(d))

    def rc_all(l):
        blocks = rr_ref.at[l, pl.ds(0, n_spot - 1)]
        return remote(blocks, blocks, r_send.at[l], r_recv.at[l], spot_peer(1))

    red_half = pl.ds(pl.multiple_of(core * 128, 128), 128)
    red_block = pl.ds(pl.multiple_of(core * 128 + spot * 16, 16), 16)

    def ac(l, d):
        return remote(red_ref.at[l, red_block, :], red_ref.at[l, red_block, :], a_send.at[l], a_recv.at[l], spot_peer(d))

    def ac_all(l):
        blocks = red_ref.at[l, pl.ds(0, 112), :]
        return remote(blocks, blocks, a_send.at[l], a_recv.at[l], spot_peer(1))

    def sc(l):
        return remote(red_ref.at[l, red_half, :], red_ref.at[l, red_half, :], s_send.at[l], s_recv.at[l], {"rays": sibling})

    def forward_weights(l):
        weights[l].wait()
        thi, tlo = split(w_ref[l].T)
        wt_ref[l] = left3(thi, tlo, 1)
        if l == 0:
            v_ref[...] = left3(thi, tlo, 0)

    def backward_weights():
        for l in range(1, LAYERS):
            wb_ref[l] = left3(*split(w_ref[l]), 1)

    def ray_inputs():
        for c in small:
            c.wait()
        headt_ref[...] = jnp.broadcast_to(head_ref[...], (GROUP, D)).T
        slot = lax.broadcasted_iota(jnp.int32, (SLOTS, GROUP), 0)
        for g in range(n_groups):
            rays = slice(g * GROUP, (g + 1) * GROUP)
            sm_ref[g, 0] = jnp.where(slot < cnt_ref[:, rays], sp_ref[:, rays], 0.0)

    def decoder_inputs():
        hi, lo = split(din_ref[...])
        dv_ref[...] = left3(hi, lo, 0)
        dh_ref[...] = left3(hi, lo, 1)
        ogs_ref[...] = jnp.zeros_like(ogs_ref)
        for g in range(n_groups):
            et_ref[...] = jnp.zeros_like(et_ref)
            et_ref[0:COLORS, :] = cg_ref[:, g * GROUP:(g + 1) * GROUP]
            cgt_ref[g] = et_ref[...].T

    def x_rows(g, s):
        return pl.ds(g * GROUP * SLOTS + s, GROUP, stride=SLOTS)

    def x_load(g, s):
        return jnp.concatenate([x_ref[side, x_rows(g, s), :] for side in range(2)], axis=1)

    def forward(g, half):
        chunk = 2 * g + half
        hidden = [None] * 4
        for q in range(4):
            slabs = [x_load(g, 8 * half + 2 * q + t) for t in range(2)]
            hidden[q] = right3(*split(jnp.concatenate(slabs, axis=0)), 1)
        for l in range(LAYERS):
            for q in range(4):
                columns = pl.ds(q * 2 * GROUP, 2 * GROUP)
                pre = mm(wt_ref[l], hidden[q], NT if l == 0 else NN)
                act, slope = silu_and_slope(pre)
                s_ref[l, chunk, :, columns] = slope
                if l < LAYERS - 1:
                    hi, lo = split(act)
                    h_ref[l, 0, chunk, :, columns] = hi
                    h_ref[l, 1, chunk, :, columns] = lo
                    hidden[q] = right3(hi, lo, 0)
                else:
                    f_ref[chunk, :, columns] = act
                    for t in range(2):
                        z = jnp.sum(act[:, t * GROUP:(t + 1) * GROUP] * headt_ref[...], axis=0, keepdims=True)
                        z_ref[g, pl.ds(8 * half + 2 * q + t, 1), :] = z

    def slot_of(ref, g, s):
        return ref[2 * g + s // 8, :, (s % 8) * GROUP:(s % 8 + 1) * GROUP]

    def rays_forward(g):
        z = z_ref[g]
        tau = softplus(z) * sm_ref[g, 0]
        incl = cumulative(tau)
        excl = incl - tau
        opaque = one_minus_exp(tau)
        sm_ref[g, 1] = tau
        sm_ref[g, 2] = excl
        sm_ref[g, 3] = opaque
        sm_ref[g, 4] = sm_ref[g, 0] * jax.nn.sigmoid(z)
        total = jnp.broadcast_to(incl[SLOTS - 1:SLOTS, :], (8, GROUP))
        t_ref[g] = total
        tr_ref[g, me] = total
        each(n_cell, functools.partial(t1, g))
        local = jnp.exp(-excl) * opaque
        acc = slot_of(f_ref, g, 0) * local[0:1, :]
        for s in range(1, SLOTS):
            acc = acc + slot_of(f_ref, g, s) * local[s:s + 1, :]
        p_ref[g] = acc.T
        each(n_cell, functools.partial(e1, g))
        pr_ref[g, me] = p_ref[g, my_rows, :]

    def decode(g):
        t1_all(g).wait_recv()
        e1_all(g).wait_recv()
        offset = jnp.zeros((1, GROUP), F32)
        own = jnp.zeros((1, GROUP), F32)
        rows = []
        for j in range(n_cell):
            rows.append(jnp.exp(-offset))
            own = jnp.where(me == j, offset, own)
            offset = offset + tr_ref[g, j][0:1, :]
        sm_ref[g, 5] = jnp.broadcast_to(own, (SLOTS, GROUP))
        et_ref[...] = jnp.concatenate(rows + [jnp.zeros((GROUP - n_cell, GROUP), F32)], axis=0).T
        et = et_ref[my_rows, :]
        parts = [pr_ref[g, j] * et[:, j:j + 1] for j in range(n_cell)]
        pixel = parts[0]
        for j in range(1, n_cell):
            pixel = pixel + parts[j]
        px_ref[g] = pixel
        pre = mm(right3(*split(pixel), 1), dv_ref[...], NN)
        colors = cgt_ref[g, my_rows, :]
        act, slope = silu_and_slope(pre)
        reach = colors[:, 0:1] * dout_ref[0:1, :]
        for c in range(1, COLORS):
            reach = reach + colors[:, c:c + 1] * dout_ref[c:c + 1, :]
        dpre = reach * slope
        dpre_ref[g] = dpre
        for c in range(COLORS):
            ogs_ref[g, c:c + 1, :] = jnp.sum(act * colors[:, c:c + 1], axis=0, keepdims=True)
        grad = mm(right3(*split(dpre), 1), dh_ref[...], NT)
        lanes = lax.broadcasted_iota(jnp.int32, (owned, GROUP), 1)
        later = jnp.zeros((owned, GROUP), F32)
        for j in range(1, n_cell):
            value = jnp.sum(parts[j] * grad, axis=1, keepdims=True)
            later = later + jnp.where(lanes < j, value, 0.0)
        payload = jnp.concatenate([grad, later], axis=1)
        qs_ref[g] = payload
        each(n_cell, functools.partial(e2, g))
        q_ref[g, my_rows, :] = payload

    def decoder_grads():
        px = right3(*split(px_ref[...].reshape(n_groups * owned, D)), 0)
        dp = left3(*split(dpre_ref[...].reshape(n_groups * owned, D)), 0)
        grad = mm(px, dp, TN)
        colors = ogs_ref[0]
        for g in range(1, n_groups):
            colors = colors + ogs_ref[g]
        for j in range(n_cell):
            igs_ref[j, 0:32, :] = grad[32 * j:32 * j + 32, :]
            igs_ref[j, 32:40, :] = colors
        each(n_cell, igc)
        igr_ref[me] = igs_ref[me]

    def rays_backward(g):
        e2_all(g).wait_recv()
        gradt = q_ref[g, :, 0:D].T
        latert = q_ref[g, :, D:D + GROUP].T[0:8, :]
        picked = lax.broadcasted_iota(jnp.int32, (8, GROUP), 0) == me
        later = jnp.sum(jnp.where(picked, latert, 0.0), axis=0, keepdims=True)
        et_ref[...] = jnp.zeros_like(et_ref)
        for s in range(SLOTS):
            et_ref[s:s + 1, :] = jnp.sum(slot_of(f_ref, g, s) * gradt, axis=0, keepdims=True)
        c = et_ref[0:SLOTS, :]
        tau = sm_ref[g, 1]
        trans = jnp.exp(-(sm_ref[g, 5] + sm_ref[g, 2]))
        weight = trans * sm_ref[g, 3]
        incl = cumulative(weight * c)
        after = later + incl[SLOTS - 1:SLOTS, :] - incl
        dz = sm_ref[g, 4] * (trans * jnp.exp(-tau) * c - after)
        sm_ref[g, 6] = weight
        sm_ref[g, 7] = dz
        q_ref[g, :, 0:GROUP] = gradt[0:GROUP, :]
        q_ref[g, :, GROUP:2 * GROUP] = gradt[GROUP:D, :]

    def head_step(chunk, l):
        g, half = chunk // 2, lax.rem(chunk, 2)
        for q in range(8):
            row = pl.ds(8 * half + q, 1)
            weight, dz = sm_ref[g, 6, row, :], sm_ref[g, 7, row, :]
            columns = pl.ds(q * GROUP, GROUP)
            for part in range(2):
                rows = pl.ds(part * 128, 128)
                back = q_ref[g, :, part * GROUP:(part + 1) * GROUP] * weight + headt_ref[rows, :] * dz
                hacc_ref[rows, :] += f_ref[chunk, rows, columns] * dz
                hi, lo = split(back * s_ref[LAYERS - 1, chunk, rows, columns])
                dph_ref[chunk, rows, columns] = hi
                dpl_ref[chunk, rows, columns] = lo

    def layer_step(chunk, l):
        hi, lo = dph_ref[chunk], dpl_ref[chunk]
        source = right3(h_ref[l - 1, 0, chunk], h_ref[l - 1, 1, chunk], 1)
        g_ref[l] += mm(source, left3(hi, lo, 1), NT)
        for q in range(4):
            columns = slice(q * 2 * GROUP, (q + 1) * 2 * GROUP)
            back = mm(wb_ref[l], right3(hi[:, columns], lo[:, columns], 0), NN)
            nhi, nlo = split(back * s_ref[l - 1, chunk, :, columns])
            dph_ref[chunk, :, columns] = nhi
            dpl_ref[chunk, :, columns] = nlo

    def first_grad(chunk):
        g, half = chunk // 2, lax.rem(chunk, 2)
        rows = jnp.concatenate([x_load(g, 8 * half + q) for q in range(8)], axis=0)
        g_ref[0] += mm(left3(dph_ref[chunk], dpl_ref[chunk], 1), right3(*split(rows), 0), NN)

    def first_back(chunk):
        g, half = chunk // 2, lax.rem(chunk, 2)
        for q in range(4):
            columns = slice(q * 2 * GROUP, (q + 1) * 2 * GROUP)
            back = mm(right3(dph_ref[chunk, :, columns], dpl_ref[chunk, :, columns], 0), v_ref[...], TN)
            for t in range(2):
                for side in range(2):
                    x_ref[side, x_rows(g, 8 * half + 2 * q + t), :] = back[
                        t * GROUP:(t + 1) * GROUP, side * 128:(side + 1) * 128
                    ]

    def sum_a(l):
        cc(l).start()

    def sum_b(l):
        cc(l).wait_recv()
        half_ref[l] = g_ref[l, red_half, :] + cr_ref[l]
        each(n_spot, functools.partial(rc, l))
        rr_ref[l, spot] = half_ref[l, pl.ds(pl.multiple_of(spot * 16, 16), 16), :]

    def sum_c(l):
        rc_all(l).wait_recv()
        total = rr_ref[l, 0]
        for j in range(1, n_spot):
            total = total + rr_ref[l, j]
        red_ref[l, red_block, :] = total
        each(n_spot, functools.partial(ac, l))

    def sum_d(l):
        ac_all(l).wait_recv()
        sc(l).start()

    def sum_e(l):
        sc(l).wait_recv()

    def extra_a():
        igc_all().wait_recv()
        total = igr_ref[0]
        for j in range(1, n_cell):
            total = total + igr_ref[j]
        ex_ref[0:40, :] = total
        ex_ref[40:48, :] = jnp.broadcast_to(jnp.sum(hacc_ref[...].T, axis=0, keepdims=True), (8, D))
        ecc().start()

    def extra_b():
        ecc().wait_recv()
        eb_ref[spot] = ex_ref[ex_mine, :] + exc_ref[...]
        each(n_spot, ebc)

    def extra_c():
        ebc_all().wait_recv()
        total = eb_ref[0]
        for j in range(1, n_spot):
            total = total + eb_ref[j]
        ef_ref[ex_mine, :] = total
        efc().start()

    def extra_d():
        efc().wait_recv()
        each(n_cell, iac)
        igf_ref[me] = ef_ref[0:32, :]

    def extra_e():
        iac_all().wait_recv()
        og_ref[...] = ef_ref[32:32 + COLORS, :]
        hg_ref[...] = ef_ref[40:41, :]

    def wait_x(g):
        for side in range(2):
            take(g, side).wait()

    def forward_loop(g):
        def body(half, _):
            forward(g, half)
            return 0

        lax.fori_loop(0, 2, body, 0)

    def rest(first_chunk, step):
        def body(chunk, _):
            step(chunk)
            return 0

        lax.fori_loop(first_chunk, first_chunk + 2, body, 0)

    def top(chunk):
        head_step(chunk, LAYERS - 1)
        layer_step(chunk, LAYERS - 1)

    middle = [functools.partial(layer_step, l=l) for l in range(LAYERS)]
    forward_weights(0)
    ray_inputs()
    for l in range(1, LAYERS):
        forward_weights(l)
    wait_x(0)
    forward_loop(0)
    pl.semaphore_wait(barrier, 2 * (n_cell - 1) + 1)
    rays_forward(0)
    wait_x(1)
    forward_loop(1)
    rays_forward(1)
    decoder_inputs()
    decode(0)
    backward_weights()
    g_ref[...] = jnp.zeros_like(g_ref)
    hacc_ref[...] = jnp.zeros_like(hacc_ref)
    rays_backward(0)
    rest(0, top)
    decode(1)
    rest(0, middle[2])
    decoder_grads()
    rest(0, middle[1])
    rays_backward(1)
    rest(2, top)
    sum_a(3)
    extra_a()
    rest(2, middle[2])
    sum_b(3)
    extra_b()
    sum_a(2)
    rest(2, middle[1])
    sum_b(2)
    sum_a(1)
    rest(0, first_grad)
    sum_b(1)
    rest(2, first_grad)
    g_ref[0] = g_ref[0].T
    sum_a(0)
    sum_c(3)
    extra_c()
    rest(0, first_back)
    sum_b(0)
    sum_c(2)
    extra_d()
    rest(2, first_back)
    sum_c(1)
    sum_d(3)
    sum_c(0)
    sum_d(2)
    sum_d(1)
    extra_e()
    sum_e(3)
    sum_e(2)
    sum_d(0)
    sum_e(1)
    sum_e(0)
    for g in range(n_groups):
        t1_all(g).wait_send()
        e1_all(g).wait_send()
        e2_all(g).wait_send()
    igc_all().wait_send()
    ecc().wait_send()
    ebc_all().wait_send()
    efc().wait_send()
    iac_all().wait_send()
    for l in range(LAYERS):
        cc(l).wait_send()
        rc_all(l).wait_send()
        ac_all(l).wait_send()
        sc(l).wait_send()


def hand_over(lg_ref, hg_ref, ig_ref, og_ref, sg_ref, lg_hbm, hg_hbm, ig_hbm, og_hbm, sg_hbm, sems):
    copies = [
        pltpu.make_async_copy(src, dst, sems.at[n])
        for n, (src, dst) in enumerate(
            ((lg_ref, lg_hbm), (hg_ref, hg_hbm), (ig_ref, ig_hbm), (og_ref, og_hbm))
        )
    ]
    for side in range(2):
        lanes = pl.ds(side * 128, 128)
        copies.append(pltpu.make_async_copy(sg_ref.at[side], sg_hbm.at[:, lanes], sems.at[4 + side]))
    for c in copies[::-1]:
        c.start()
    for c in copies:
        c.wait()


def local(n_cell, encodings, spacing, counts, cell_weights, density_head, decoder_in, decoder_out, color_grad):
    rays, slots, width = encodings.shape
    rows = rays * slots
    groups, chunks, wide = rays // GROUP, rows // (8 * GROUP), 8 * GROUP
    owned = GROUP // n_cell
    vmem = pl.BlockSpec(memory_space=pltpu.VMEM)
    anywhere = pl.BlockSpec(memory_space=pl.ANY)
    dma = pltpu.SemaphoreType.DMA
    V = pltpu.VMEM
    scratch = [
        V((slots, rays), F32),
        V((1, rays), jnp.int32),
        V((LAYERS, D, D), F32),
        V((1, D), F32),
        V((D, D), F32),
        V((COLORS, D), F32),
        V((COLORS, rays), F32),
        V((groups, GROUP, GROUP), F32),
        V((LAYERS - 1, 2, chunks, D, wide), BF16),
        V((LAYERS, chunks, D, wide), F32),
        V((chunks, D, wide), F32),
        V((chunks, D, wide), BF16),
        V((chunks, D, wide), BF16),
        V((LAYERS, D, 3 * D), BF16),
        V((LAYERS, D, 3 * D), BF16),
        V((3 * D, D), BF16),
        V((3 * D, D), BF16),
        V((D, 3 * D), BF16),
        V((D, GROUP), F32),
        V((groups, SLOTS, GROUP), F32),
        V((groups, 8, SLOTS, GROUP), F32),
        V((GROUP, GROUP), F32),
        V((D, GROUP), F32),
        V((groups, GROUP, D), F32),
        V((groups, n_cell, owned, D), F32),
        V((groups, 8, GROUP), F32),
        V((groups, n_cell, 8, GROUP), F32),
        V((groups, GROUP, D + GROUP), F32),
        V((groups, owned, D + GROUP), F32),
        V((groups, owned, D), F32),
        V((groups, owned, D), F32),
        V((groups, 8, D), F32),
        V((n_cell, 40, D), F32),
        V((n_cell, 40, D), F32),
        V((48, D), F32),
        V((24, D), F32),
        V((8, 24, D), F32),
        V((48, D), F32),
        V((LAYERS, D, D), F32),
        V((LAYERS, 128, D), F32),
        V((LAYERS, 128, D), F32),
        V((LAYERS, 8, 16, D), F32),
        dma((groups, 2)), dma((6 + LAYERS,)),
        dma((groups,)), dma((groups,)),
        dma((groups,)), dma((groups,)),
        dma((groups,)), dma((groups,)),
        dma((1,)), dma((1,)),
        dma((1,)), dma((1,)),
        dma((1,)), dma((1,)),
        dma((1,)), dma((1,)),
        dma((1,)), dma((1,)),
        dma((LAYERS,)), dma((LAYERS,)),
        dma((LAYERS,)), dma((LAYERS,)),
        dma((LAYERS,)), dma((LAYERS,)),
        dma((LAYERS,)), dma((LAYERS,)),
    ]
    outs = [V((LAYERS, D, D), F32), V((1, D), F32), V((n_cell, 32, D), F32), V((COLORS, D), F32), V((2, rows, 128), F32)]
    parts = pl.pallas_call(
        functools.partial(kernel, n_cell),
        out_shape=outs,
        in_specs=[anywhere] * 8,
        out_specs=[vmem] * 5,
        scratch_shapes=scratch,
        compiler_params=pltpu.CompilerParams(
            collective_id=0, has_side_effects=True, vmem_limit_bytes=56 << 20
        ),
    )(
        encodings.reshape(rows, width), spacing.T, counts.T, cell_weights[0], density_head,
        decoder_in, decoder_out.T, color_grad.T,
    )
    layer, head, din, dout, sample = pl.pallas_call(
        hand_over,
        out_shape=[
            jax.ShapeDtypeStruct((LAYERS, D, D), F32),
            jax.ShapeDtypeStruct((1, D), F32),
            jax.ShapeDtypeStruct((n_cell, 32, D), F32),
            jax.ShapeDtypeStruct((COLORS, D), F32),
            jax.ShapeDtypeStruct((rows, D), F32),
        ],
        in_specs=[vmem] * 5,
        out_specs=[anywhere] * 5,
        scratch_shapes=[dma((6,))],
        compiler_params=pltpu.CompilerParams(vmem_limit_bytes=1 << 20),
    )(*(pltpu.with_memory_space_constraint(part, pltpu.VMEM) for part in parts))
    return layer[None], head, din.reshape(D, D), dout.T, sample.reshape(rays, slots, width)


def solution(mesh):
    return jax.shard_map(
        functools.partial(local, mesh.shape["cell"]),
        mesh=mesh,
        in_specs=(
            P("rays", "cell", None), P("rays", "cell"), P("rays", "cell"), P("cell", None, None, None),
            P("cell", None), P(None, None), P(None, None), P("rays", None),
        ),
        out_specs=(
            P("cell", None, None, None), P("cell", None), P(None, None), P(None, None), P("rays", "cell", None),
        ),
        check_vma=False,
    )
```

```python
import functools

import jax
import jax.numpy as jnp
from jax import lax
from jax.experimental import pallas as pl
from jax.experimental.pallas import tpu as pltpu
from jax.sharding import PartitionSpec as P

F32, BF16 = jnp.float32, jnp.bfloat16
D, LAYERS, SLOTS, COLORS = 256, 4, 16, 3
GROUP = 128
NT = (((1,), (1,)), ((), ()))
NN = (((1,), (0,)), ((), ()))
TN = (((0,), (0,)), ((), ()))


def mm(a, b, dims):
    return lax.dot_general(a, b, dims, preferred_element_type=F32)


def split(v):
    hi = v.astype(BF16)
    return hi, (v - hi.astype(F32)).astype(BF16)


def left3(hi, lo, axis):
    return jnp.concatenate([hi, hi, lo], axis=axis)


def right3(hi, lo, axis):
    return jnp.concatenate([hi, lo, hi], axis=axis)


def silu_and_slope(pre):
    sig = jax.nn.sigmoid(pre)
    act = pre * sig
    return act, sig + act * (1.0 - sig)


def softplus(z):
    y = jnp.exp(-jnp.abs(z))
    s = y / (2.0 + y)
    q = s * s
    series = 1.0 / 17.0
    for odd in (15, 13, 11, 9, 7, 5, 3, 1):
        series = series * q + 1.0 / odd
    return jnp.maximum(z, 0.0) + 2.0 * s * series


def one_minus_exp(tau):
    series = 1.0
    for k in (7, 6, 5, 4, 3, 2):
        series = 1.0 - tau * series * (1.0 / k)
    return jnp.where(tau < 0.25, tau * series, 1.0 - jnp.exp(-tau))


def cumulative(v):
    rows = lax.broadcasted_iota(jnp.int32, v.shape, 0)
    for step in (1, 2, 4, 8):
        v = v + jnp.where(rows >= step, pltpu.roll(v, step, 0), 0.0)
    return v


def kernel(
    n_cell, x_hbm, sp_hbm, cnt_hbm, w_hbm, head_hbm, din_hbm, dout_hbm, cg_hbm,
    red_ref, hg_ref, igf_ref, og_ref, x_ref,
    sp_ref, cnt_ref, w_ref, head_ref, din_ref, dout_ref, cg_ref, cgt_ref,
    h_ref, s_ref, f_ref, dph_ref, dpl_ref,
    wt_ref, wb_ref, v_ref, dv_ref, dh_ref, headt_ref,
    z_ref, sm_ref, et_ref, hacc_ref,
    p_ref, pr_ref, t_ref, tr_ref, q_ref, qs_ref, px_ref, dpre_ref, ogs_ref,
    igs_ref, igr_ref, ex_ref, exc_ref, eb_ref, ef_ref, hx_ref, xs_ref,
    g_ref, cr_ref, half_ref, rr_ref,
    x_sem, in_sem, e1_send, e1_recv, t_send, t_recv, e2_send, e2_recv,
    ig_send, ig_recv, ec_send, ec_recv, eb_send, eb_recv, ef_send, ef_recv, ia_send, ia_recv, hx_send, hx_recv,
    c_send, c_recv, r_send, r_recv, a_send, a_recv, s_send, s_recv,
):
    me = lax.axis_index("cell")
    ray = lax.axis_index("rays")
    core = lax.rem(ray, 2)
    spot = ray // 2
    sibling = ray + 1 - 2 * core
    n_groups = sp_ref.shape[1] // GROUP
    n_spot = 8
    owned = GROUP // n_cell
    wide = 8 * GROUP
    my_rows = pl.ds(pl.multiple_of(me * owned, 8), owned)

    def take(g, side):
        part = pl.ds(g * GROUP * SLOTS, GROUP * SLOTS)
        lanes = pl.ds(side * 128, 128)
        return pltpu.make_async_copy(x_hbm.at[part, lanes], x_ref.at[side, part, :], x_sem.at[g, side])

    pairs = (
        (head_hbm, head_ref), (sp_hbm, sp_ref), (cnt_hbm, cnt_ref), (cg_hbm, cg_ref), (dout_hbm, dout_ref),
        (din_hbm, din_ref),
    )
    small = [pltpu.make_async_copy(src, dst, in_sem.at[n]) for n, (src, dst) in enumerate(pairs)]
    weights = [
        pltpu.make_async_copy(w_hbm.at[l], w_ref.at[l], in_sem.at[len(pairs) + l]) for l in range(LAYERS)
    ]
    weights[0].start()
    for g in range(n_groups):
        for side in range(2):
            take(g, side).start()
        if g == 0:
            for c in weights[1:] + small:
                c.start()

    def cell_peer(d):
        return {"cell": lax.rem(me + d, n_cell)}

    def spot_peer(d):
        return {"rays": 2 * lax.rem(spot + d, n_spot) + core}

    def ray_peer(d):
        return {"rays": lax.rem(ray + d, 2 * n_spot)}

    barrier = pltpu.get_barrier_semaphore()

    def greet(d, _):
        pl.semaphore_signal(barrier, inc=1, device_id=cell_peer(d))
        return 0

    def greet_rays(d, _):
        pl.semaphore_signal(barrier, inc=1, device_id=ray_peer(d))
        return 0

    lax.fori_loop(1, n_cell, greet, 0)
    lax.fori_loop(1, 2 * n_spot, greet_rays, 0)

    def remote(src, dst, send, recv, device):
        return pltpu.make_async_remote_copy(
            src_ref=src, dst_ref=dst, send_sem=send, recv_sem=recv, device_id=device
        )

    def each(count, make):
        def body(d, _):
            make(d).start()
            return 0

        lax.fori_loop(1, count, body, 0)

    def e1(g, d):
        to = lax.rem(me + d, n_cell)
        rows = pl.ds(pl.multiple_of(to * owned, 8), owned)
        return remote(p_ref.at[g, rows, :], pr_ref.at[g, me], e1_send.at[g], e1_recv.at[g], cell_peer(d))

    def e1_all(g):
        blocks = pr_ref.at[g, pl.ds(0, n_cell - 1)]
        return remote(blocks, blocks, e1_send.at[g], e1_recv.at[g], cell_peer(1))

    def t1(g, d):
        return remote(t_ref.at[g], tr_ref.at[g, me], t_send.at[g], t_recv.at[g], cell_peer(d))

    def t1_all(g):
        blocks = tr_ref.at[g, pl.ds(0, n_cell - 1)]
        return remote(blocks, blocks, t_send.at[g], t_recv.at[g], cell_peer(1))

    def e2(g, d):
        return remote(qs_ref.at[g], q_ref.at[g, my_rows, :], e2_send.at[g], e2_recv.at[g], cell_peer(d))

    def e2_all(g):
        blocks = q_ref.at[g, pl.ds(0, GROUP - owned), :]
        return remote(blocks, blocks, e2_send.at[g], e2_recv.at[g], cell_peer(1))

    def igc(d):
        to = lax.rem(me + d, n_cell)
        return remote(igs_ref.at[to], igr_ref.at[me], ig_send.at[0], ig_recv.at[0], cell_peer(d))

    def igc_all():
        blocks = igr_ref.at[pl.ds(0, n_cell - 1)]
        return remote(blocks, blocks, ig_send.at[0], ig_recv.at[0], cell_peer(1))

    ex_mine = pl.ds(pl.multiple_of(core * 24, 8), 24)
    ex_other = pl.ds(pl.multiple_of((1 - core) * 24, 8), 24)

    def ecc():
        return remote(ex_ref.at[ex_other, :], exc_ref, ec_send.at[0], ec_recv.at[0], {"rays": sibling})

    def ebc(d):
        return remote(eb_ref.at[spot], eb_ref.at[spot], eb_send.at[0], eb_recv.at[0], spot_peer(d))

    def ebc_all():
        blocks = eb_ref.at[pl.ds(0, n_spot - 1)]
        return remote(blocks, blocks, eb_send.at[0], eb_recv.at[0], spot_peer(1))

    def efc():
        return remote(ef_ref.at[ex_mine, :], ef_ref.at[ex_mine, :], ef_send.at[0], ef_recv.at[0], {"rays": sibling})

    def iac(d):
        return remote(ef_ref.at[pl.ds(0, 32), :], igf_ref.at[me], ia_send.at[0], ia_recv.at[0], cell_peer(d))

    def iac_all():
        blocks = igf_ref.at[pl.ds(0, n_cell - 1)]
        return remote(blocks, blocks, ia_send.at[0], ia_recv.at[0], cell_peer(1))

    def hx(d):
        return remote(hx_ref.at[ray], hx_ref.at[ray], hx_send.at[0], hx_recv.at[0], ray_peer(d))

    def hx_all():
        blocks = hx_ref.at[pl.ds(0, 2 * n_spot - 1)]
        return remote(blocks, blocks, hx_send.at[0], hx_recv.at[0], ray_peer(1))

    def cc(l):
        other = pl.ds(pl.multiple_of((1 - core) * 128, 128), 128)
        return remote(g_ref.at[l, other, :], cr_ref.at[l], c_send.at[l], c_recv.at[l], {"rays": sibling})

    def rc(l, d):
        to = lax.rem(spot + d, n_spot)
        rows = pl.ds(pl.multiple_of(to * 16, 16), 16)
        return remote(half_ref.at[l, rows, :], rr_ref.at[l, spot], r_send.at[l], r_recv.at[l], spot_peer(d))

    def rc_all(l):
        blocks = rr_ref.at[l, pl.ds(0, n_spot - 1)]
        return remote(blocks, blocks, r_send.at[l], r_recv.at[l], spot_peer(1))

    red_half = pl.ds(pl.multiple_of(core * 128, 128), 128)
    red_block = pl.ds(pl.multiple_of(core * 128 + spot * 16, 16), 16)

    def ac(l, d):
        return remote(red_ref.at[l, red_block, :], red_ref.at[l, red_block, :], a_send.at[l], a_recv.at[l], spot_peer(d))

    def ac_all(l):
        blocks = red_ref.at[l, pl.ds(0, 112), :]
        return remote(blocks, blocks, a_send.at[l], a_recv.at[l], spot_peer(1))

    def sc(l):
        return remote(red_ref.at[l, red_half, :], red_ref.at[l, red_half, :], s_send.at[l], s_recv.at[l], {"rays": sibling})

    def forward_weights(l):
        weights[l].wait()
        thi, tlo = split(w_ref[l].T)
        wt_ref[l] = left3(thi, tlo, 1)
        if l == 0:
            v_ref[...] = left3(thi, tlo, 0)

    def backward_weights():
        for l in range(1, LAYERS):
            wb_ref[l] = left3(*split(w_ref[l]), 1)

    def ray_inputs():
        for c in small:
            c.wait()
        headt_ref[...] = jnp.broadcast_to(head_ref[...], (GROUP, D)).T
        slot = lax.broadcasted_iota(jnp.int32, (SLOTS, GROUP), 0)
        for g in range(n_groups):
            rays = slice(g * GROUP, (g + 1) * GROUP)
            sm_ref[g, 0] = jnp.where(slot < cnt_ref[:, rays], sp_ref[:, rays], 0.0)

    def decoder_inputs():
        hi, lo = split(din_ref[...])
        dv_ref[...] = left3(hi, lo, 0)
        dh_ref[...] = left3(hi, lo, 1)
        ogs_ref[...] = jnp.zeros_like(ogs_ref)
        for g in range(n_groups):
            et_ref[...] = jnp.zeros_like(et_ref)
            et_ref[0:COLORS, :] = cg_ref[:, g * GROUP:(g + 1) * GROUP]
            cgt_ref[g] = et_ref[...].T

    def x_rows(g, s):
        return pl.ds(g * GROUP * SLOTS + s, GROUP, stride=SLOTS)

    def x_load(g, s):
        return jnp.concatenate([x_ref[side, x_rows(g, s), :] for side in range(2)], axis=1)

    def forward(g, half):
        chunk = 2 * g + half
        hidden = [None] * 4
        for q in range(4):
            slabs = [x_load(g, 8 * half + 2 * q + t) for t in range(2)]
            hidden[q] = right3(*split(jnp.concatenate(slabs, axis=0)), 1)
        for l in range(LAYERS):
            for q in range(4):
                columns = pl.ds(q * 2 * GROUP, 2 * GROUP)
                pre = mm(wt_ref[l], hidden[q], NT if l == 0 else NN)
                act, slope = silu_and_slope(pre)
                s_ref[l, chunk, :, columns] = slope
                if l < LAYERS - 1:
                    hi, lo = split(act)
                    h_ref[l, 0, chunk, :, columns] = hi
                    h_ref[l, 1, chunk, :, columns] = lo
                    hidden[q] = right3(hi, lo, 0)
                else:
                    f_ref[chunk, :, columns] = act
                    for t in range(2):
                        z = jnp.sum(act[:, t * GROUP:(t + 1) * GROUP] * headt_ref[...], axis=0, keepdims=True)
                        z_ref[g, pl.ds(8 * half + 2 * q + t, 1), :] = z

    def slot_of(ref, g, s):
        return ref[2 * g + s // 8, :, (s % 8) * GROUP:(s % 8 + 1) * GROUP]

    def rays_forward(g):
        z = z_ref[g]
        tau = softplus(z) * sm_ref[g, 0]
        incl = cumulative(tau)
        excl = incl - tau
        opaque = one_minus_exp(tau)
        sm_ref[g, 1] = tau
        sm_ref[g, 2] = excl
        sm_ref[g, 3] = opaque
        sm_ref[g, 4] = sm_ref[g, 0] * jax.nn.sigmoid(z)
        total = jnp.broadcast_to(incl[SLOTS - 1:SLOTS, :], (8, GROUP))
        t_ref[g] = total
        tr_ref[g, me] = total
        each(n_cell, functools.partial(t1, g))
        local = jnp.exp(-excl) * opaque
        acc = slot_of(f_ref, g, 0) * local[0:1, :]
        for s in range(1, SLOTS):
            acc = acc + slot_of(f_ref, g, s) * local[s:s + 1, :]
        p_ref[g] = acc.T
        each(n_cell, functools.partial(e1, g))
        pr_ref[g, me] = p_ref[g, my_rows, :]

    def decode(g):
        t1_all(g).wait_recv()
        e1_all(g).wait_recv()
        offset = jnp.zeros((1, GROUP), F32)
        own = jnp.zeros((1, GROUP), F32)
        rows = []
        for j in range(n_cell):
            rows.append(jnp.exp(-offset))
            own = jnp.where(me == j, offset, own)
            offset = offset + tr_ref[g, j][0:1, :]
        sm_ref[g, 5] = jnp.broadcast_to(own, (SLOTS, GROUP))
        et_ref[...] = jnp.concatenate(rows + [jnp.zeros((GROUP - n_cell, GROUP), F32)], axis=0).T
        et = et_ref[my_rows, :]
        parts = [pr_ref[g, j] * et[:, j:j + 1] for j in range(n_cell)]
        pixel = parts[0]
        for j in range(1, n_cell):
            pixel = pixel + parts[j]
        px_ref[g] = pixel
        pre = mm(right3(*split(pixel), 1), dv_ref[...], NN)
        colors = cgt_ref[g, my_rows, :]
        act, slope = silu_and_slope(pre)
        reach = colors[:, 0:1] * dout_ref[0:1, :]
        for c in range(1, COLORS):
            reach = reach + colors[:, c:c + 1] * dout_ref[c:c + 1, :]
        dpre = reach * slope
        dpre_ref[g] = dpre
        for c in range(COLORS):
            ogs_ref[g, c:c + 1, :] = jnp.sum(act * colors[:, c:c + 1], axis=0, keepdims=True)
        grad = mm(right3(*split(dpre), 1), dh_ref[...], NT)
        lanes = lax.broadcasted_iota(jnp.int32, (owned, GROUP), 1)
        later = jnp.zeros((owned, GROUP), F32)
        for j in range(1, n_cell):
            value = jnp.sum(parts[j] * grad, axis=1, keepdims=True)
            later = later + jnp.where(lanes < j, value, 0.0)
        payload = jnp.concatenate([grad, later], axis=1)
        qs_ref[g] = payload
        each(n_cell, functools.partial(e2, g))
        q_ref[g, my_rows, :] = payload

    def decoder_grads():
        px = right3(*split(px_ref[...].reshape(n_groups * owned, D)), 0)
        dp = left3(*split(dpre_ref[...].reshape(n_groups * owned, D)), 0)
        grad = mm(px, dp, TN)
        colors = ogs_ref[0]
        for g in range(1, n_groups):
            colors = colors + ogs_ref[g]
        for j in range(n_cell):
            igs_ref[j, 0:32, :] = grad[32 * j:32 * j + 32, :]
            igs_ref[j, 32:40, :] = colors
        each(n_cell, igc)
        igr_ref[me] = igs_ref[me]

    def rays_backward(g):
        e2_all(g).wait_recv()
        gradt = q_ref[g, :, 0:D].T
        latert = q_ref[g, :, D:D + GROUP].T[0:8, :]
        picked = lax.broadcasted_iota(jnp.int32, (8, GROUP), 0) == me
        later = jnp.sum(jnp.where(picked, latert, 0.0), axis=0, keepdims=True)
        et_ref[...] = jnp.zeros_like(et_ref)
        for s in range(SLOTS):
            et_ref[s:s + 1, :] = jnp.sum(slot_of(f_ref, g, s) * gradt, axis=0, keepdims=True)
        c = et_ref[0:SLOTS, :]
        tau = sm_ref[g, 1]
        trans = jnp.exp(-(sm_ref[g, 5] + sm_ref[g, 2]))
        weight = trans * sm_ref[g, 3]
        incl = cumulative(weight * c)
        after = later + incl[SLOTS - 1:SLOTS, :] - incl
        dz = sm_ref[g, 4] * (trans * jnp.exp(-tau) * c - after)
        sm_ref[g, 6] = weight
        sm_ref[g, 7] = dz
        q_ref[g, :, 0:GROUP] = gradt[0:GROUP, :]
        q_ref[g, :, GROUP:2 * GROUP] = gradt[GROUP:D, :]

    def head_step(chunk, l):
        g, half = chunk // 2, lax.rem(chunk, 2)
        for q in range(8):
            row = pl.ds(8 * half + q, 1)
            weight, dz = sm_ref[g, 6, row, :], sm_ref[g, 7, row, :]
            columns = pl.ds(q * GROUP, GROUP)
            for part in range(2):
                rows = pl.ds(part * 128, 128)
                back = q_ref[g, :, part * GROUP:(part + 1) * GROUP] * weight + headt_ref[rows, :] * dz
                hacc_ref[rows, :] += f_ref[chunk, rows, columns] * dz
                hi, lo = split(back * s_ref[LAYERS - 1, chunk, rows, columns])
                dph_ref[chunk, rows, columns] = hi
                dpl_ref[chunk, rows, columns] = lo

    def layer_step(chunk, l):
        hi, lo = dph_ref[chunk], dpl_ref[chunk]
        source = right3(h_ref[l - 1, 0, chunk], h_ref[l - 1, 1, chunk], 1)
        g_ref[l] += mm(source, left3(hi, lo, 1), NT)
        for q in range(4):
            columns = slice(q * 2 * GROUP, (q + 1) * 2 * GROUP)
            back = mm(wb_ref[l], right3(hi[:, columns], lo[:, columns], 0), NN)
            nhi, nlo = split(back * s_ref[l - 1, chunk, :, columns])
            dph_ref[chunk, :, columns] = nhi
            dpl_ref[chunk, :, columns] = nlo

    def x_split(chunk):
        g, half = chunk // 2, lax.rem(chunk, 2)
        for q in range(8):
            hi, lo = split(x_load(g, 8 * half + q))
            xs_ref[0, chunk, q * GROUP:(q + 1) * GROUP, :] = hi
            xs_ref[1, chunk, q * GROUP:(q + 1) * GROUP, :] = lo

    def first_grad(chunk):
        rows = right3(xs_ref[0, chunk], xs_ref[1, chunk], 0)
        g_ref[0] += mm(left3(dph_ref[chunk], dpl_ref[chunk], 1), rows, NN)

    def first_back(chunk):
        g, half = chunk // 2, lax.rem(chunk, 2)
        for q in range(4):
            columns = slice(q * 2 * GROUP, (q + 1) * 2 * GROUP)
            back = mm(right3(dph_ref[chunk, :, columns], dpl_ref[chunk, :, columns], 0), v_ref[...], TN)
            for t in range(2):
                for side in range(2):
                    x_ref[side, x_rows(g, 8 * half + 2 * q + t), :] = back[
                        t * GROUP:(t + 1) * GROUP, side * 128:(side + 1) * 128
                    ]

    def sum_a(l):
        cc(l).start()

    def sum_b(l):
        cc(l).wait_recv()
        half_ref[l] = g_ref[l, red_half, :] + cr_ref[l]
        each(n_spot, functools.partial(rc, l))
        rr_ref[l, spot] = half_ref[l, pl.ds(pl.multiple_of(spot * 16, 16), 16), :]

    def sum_c(l):
        rc_all(l).wait_recv()
        total = rr_ref[l, 0]
        for j in range(1, n_spot):
            total = total + rr_ref[l, j]
        red_ref[l, red_block, :] = total
        each(n_spot, functools.partial(ac, l))

    def sum_d(l):
        ac_all(l).wait_recv()
        sc(l).start()

    def sum_e(l):
        sc(l).wait_recv()

    def extra_a():
        igc_all().wait_recv()
        total = igr_ref[0]
        for j in range(1, n_cell):
            total = total + igr_ref[j]
        ex_ref[0:40, :] = total
        ecc().start()

    def extra_b():
        ecc().wait_recv()
        eb_ref[spot] = ex_ref[ex_mine, :] + exc_ref[...]
        each(n_spot, ebc)

    def extra_c():
        ebc_all().wait_recv()
        total = eb_ref[0]
        for j in range(1, n_spot):
            total = total + eb_ref[j]
        ef_ref[ex_mine, :] = total
        efc().start()

    def extra_d():
        efc().wait_recv()
        each(n_cell, iac)
        igf_ref[me] = ef_ref[0:32, :]

    def extra_e():
        iac_all().wait_recv()
        og_ref[...] = ef_ref[32:32 + COLORS, :]

    def head_a():
        hx_ref[ray] = jnp.broadcast_to(jnp.sum(hacc_ref[...].T, axis=0, keepdims=True), (8, D))
        each(2 * n_spot, hx)

    def head_b():
        hx_all().wait_recv()
        total = hx_ref[0]
        for j in range(1, 2 * n_spot):
            total = total + hx_ref[j]
        hg_ref[...] = total[0:1, :]

    def wait_x(g):
        for side in range(2):
            take(g, side).wait()

    def forward_loop(g):
        def body(half, _):
            forward(g, half)
            return 0

        lax.fori_loop(0, 2, body, 0)

    def rest(first_chunk, step, between=None):
        def body(chunk, _):
            step(chunk)
            if between is not None:
                pl.when(chunk == first_chunk)(between)
            return 0

        lax.fori_loop(first_chunk, first_chunk + 2, body, 0)

    def top(chunk):
        head_step(chunk, LAYERS - 1)
        layer_step(chunk, LAYERS - 1)

    middle = [functools.partial(layer_step, l=l) for l in range(LAYERS)]
    forward_weights(0)
    ray_inputs()
    for l in range(1, LAYERS):
        forward_weights(l)
    wait_x(0)
    forward_loop(0)
    pl.semaphore_wait(barrier, n_cell - 1 + 2 * n_spot - 1)
    rays_forward(0)
    wait_x(1)
    forward_loop(1)
    rays_forward(1)
    decoder_inputs()
    decode(0)
    backward_weights()
    g_ref[...] = jnp.zeros_like(g_ref)
    hacc_ref[...] = jnp.zeros_like(hacc_ref)
    ex_ref[40:48, :] = jnp.zeros((8, D), F32)
    rest(0, x_split)
    rest(2, x_split)
    decode(1)
    decoder_grads()
    rays_backward(0)
    rest(0, top)
    rest(0, middle[2])
    rays_backward(1)
    extra_a()
    rest(2, top, extra_b)
    sum_a(3)
    head_a()

    rest(2, middle[2], lambda: sum_b(3))
    sum_a(2)
    rest(0, middle[1], lambda: sum_b(2))
    rest(2, middle[1], extra_c)
    sum_a(1)
    extra_d()

    def sums_b1_c3():
        sum_b(1)
        sum_c(3)

    rest(0, first_grad, sums_b1_c3)
    rest(2, first_grad)
    g_ref[0] = g_ref[0].T
    sum_a(0)
    rest(0, first_back, lambda: sum_b(0))
    sum_c(2)
    rest(2, first_back)
    sum_c(1)
    sum_d(3)
    head_b()
    sum_c(0)
    sum_d(2)
    extra_e()
    sum_d(1)
    sum_e(3)
    sum_e(2)
    sum_d(0)
    sum_e(1)
    sum_e(0)
    for g in range(n_groups):
        t1_all(g).wait_send()
        e1_all(g).wait_send()
        e2_all(g).wait_send()
    igc_all().wait_send()
    ecc().wait_send()
    ebc_all().wait_send()
    efc().wait_send()
    iac_all().wait_send()
    hx_all().wait_send()
    for l in range(LAYERS):
        cc(l).wait_send()
        rc_all(l).wait_send()
        ac_all(l).wait_send()
        sc(l).wait_send()


def hand_over(lg_ref, hg_ref, ig_ref, og_ref, sg_ref, lg_hbm, hg_hbm, ig_hbm, og_hbm, sg_hbm, sems):
    copies = [
        pltpu.make_async_copy(src, dst, sems.at[n])
        for n, (src, dst) in enumerate(
            ((lg_ref, lg_hbm), (hg_ref, hg_hbm), (ig_ref, ig_hbm), (og_ref, og_hbm))
        )
    ]
    for side in range(2):
        lanes = pl.ds(side * 128, 128)
        copies.append(pltpu.make_async_copy(sg_ref.at[side], sg_hbm.at[:, lanes], sems.at[4 + side]))
    for c in copies[::-1]:
        c.start()
    for c in copies:
        c.wait()


def local(n_cell, encodings, spacing, counts, cell_weights, density_head, decoder_in, decoder_out, color_grad):
    rays, slots, width = encodings.shape
    rows = rays * slots
    groups, chunks, wide = rays // GROUP, rows // (8 * GROUP), 8 * GROUP
    owned = GROUP // n_cell
    vmem = pl.BlockSpec(memory_space=pltpu.VMEM)
    anywhere = pl.BlockSpec(memory_space=pl.ANY)
    dma = pltpu.SemaphoreType.DMA
    V = pltpu.VMEM
    scratch = [
        V((slots, rays), F32),
        V((1, rays), jnp.int32),
        V((LAYERS, D, D), F32),
        V((1, D), F32),
        V((D, D), F32),
        V((COLORS, D), F32),
        V((COLORS, rays), F32),
        V((groups, GROUP, GROUP), F32),
        V((LAYERS - 1, 2, chunks, D, wide), BF16),
        V((LAYERS, chunks, D, wide), F32),
        V((chunks, D, wide), F32),
        V((chunks, D, wide), BF16),
        V((chunks, D, wide), BF16),
        V((LAYERS, D, 3 * D), BF16),
        V((LAYERS, D, 3 * D), BF16),
        V((3 * D, D), BF16),
        V((3 * D, D), BF16),
        V((D, 3 * D), BF16),
        V((D, GROUP), F32),
        V((groups, SLOTS, GROUP), F32),
        V((groups, 8, SLOTS, GROUP), F32),
        V((GROUP, GROUP), F32),
        V((D, GROUP), F32),
        V((groups, GROUP, D), F32),
        V((groups, n_cell, owned, D), F32),
        V((groups, 8, GROUP), F32),
        V((groups, n_cell, 8, GROUP), F32),
        V((groups, GROUP, D + GROUP), F32),
        V((groups, owned, D + GROUP), F32),
        V((groups, owned, D), F32),
        V((groups, owned, D), F32),
        V((groups, 8, D), F32),
        V((n_cell, 40, D), F32),
        V((n_cell, 40, D), F32),
        V((48, D), F32),
        V((24, D), F32),
        V((8, 24, D), F32),
        V((48, D), F32),
        V((16, 8, D), F32),
        V((2, chunks, wide, D), BF16),
        V((LAYERS, D, D), F32),
        V((LAYERS, 128, D), F32),
        V((LAYERS, 128, D), F32),
        V((LAYERS, 8, 16, D), F32),
        dma((groups, 2)), dma((6 + LAYERS,)),
        dma((groups,)), dma((groups,)),
        dma((groups,)), dma((groups,)),
        dma((groups,)), dma((groups,)),
        dma((1,)), dma((1,)),
        dma((1,)), dma((1,)),
        dma((1,)), dma((1,)),
        dma((1,)), dma((1,)),
        dma((1,)), dma((1,)),
        dma((1,)), dma((1,)),
        dma((LAYERS,)), dma((LAYERS,)),
        dma((LAYERS,)), dma((LAYERS,)),
        dma((LAYERS,)), dma((LAYERS,)),
        dma((LAYERS,)), dma((LAYERS,)),
    ]
    outs = [V((LAYERS, D, D), F32), V((1, D), F32), V((n_cell, 32, D), F32), V((COLORS, D), F32), V((2, rows, 128), F32)]
    parts = pl.pallas_call(
        functools.partial(kernel, n_cell),
        out_shape=outs,
        in_specs=[anywhere] * 8,
        out_specs=[vmem] * 5,
        scratch_shapes=scratch,
        compiler_params=pltpu.CompilerParams(
            collective_id=0, has_side_effects=True, vmem_limit_bytes=56 << 20
        ),
    )(
        encodings.reshape(rows, width), spacing.T, counts.T, cell_weights[0], density_head,
        decoder_in, decoder_out.T, color_grad.T,
    )
    layer, head, din, dout, sample = pl.pallas_call(
        hand_over,
        out_shape=[
            jax.ShapeDtypeStruct((LAYERS, D, D), F32),
            jax.ShapeDtypeStruct((1, D), F32),
            jax.ShapeDtypeStruct((n_cell, 32, D), F32),
            jax.ShapeDtypeStruct((COLORS, D), F32),
            jax.ShapeDtypeStruct((rows, D), F32),
        ],
        in_specs=[vmem] * 5,
        out_specs=[anywhere] * 5,
        scratch_shapes=[dma((6,))],
        compiler_params=pltpu.CompilerParams(vmem_limit_bytes=1 << 20),
    )(*(pltpu.with_memory_space_constraint(part, pltpu.VMEM) for part in parts))
    return layer[None], head, din.reshape(D, D), dout.T, sample.reshape(rays, slots, width)


def solution(mesh):
    return jax.shard_map(
        functools.partial(local, mesh.shape["cell"]),
        mesh=mesh,
        in_specs=(
            P("rays", "cell", None), P("rays", "cell"), P("rays", "cell"), P("cell", None, None, None),
            P("cell", None), P(None, None), P(None, None), P("rays", None),
        ),
        out_specs=(
            P("cell", None, None, None), P("cell", None), P(None, None), P(None, None), P("rays", "cell", None),
        ),
        check_vma=False,
    )
```

```python
import functools

import jax
import jax.numpy as jnp
from jax import lax
from jax.experimental import pallas as pl
from jax.experimental.pallas import tpu as pltpu
from jax.sharding import PartitionSpec as P

F32, BF16 = jnp.float32, jnp.bfloat16
D, LAYERS, SLOTS, COLORS = 256, 4, 16, 3
GROUP = 128
NT = (((1,), (1,)), ((), ()))
NN = (((1,), (0,)), ((), ()))
TN = (((0,), (0,)), ((), ()))


def mm(a, b, dims):
    return lax.dot_general(a, b, dims, preferred_element_type=F32)


def split(v):
    hi = v.astype(BF16)
    return hi, (v - hi.astype(F32)).astype(BF16)


def left3(hi, lo, axis):
    return jnp.concatenate([hi, hi, lo], axis=axis)


def right3(hi, lo, axis):
    return jnp.concatenate([hi, lo, hi], axis=axis)


def silu_and_slope(pre):
    sig = jax.nn.sigmoid(pre)
    act = pre * sig
    return act, sig + act * (1.0 - sig)


def softplus(z):
    y = jnp.exp(-jnp.abs(z))
    s = y / (2.0 + y)
    q = s * s
    series = 1.0 / 17.0
    for odd in (15, 13, 11, 9, 7, 5, 3, 1):
        series = series * q + 1.0 / odd
    return jnp.maximum(z, 0.0) + 2.0 * s * series


def one_minus_exp(tau):
    series = 1.0
    for k in (7, 6, 5, 4, 3, 2):
        series = 1.0 - tau * series * (1.0 / k)
    return jnp.where(tau < 0.25, tau * series, 1.0 - jnp.exp(-tau))


def cumulative(v):
    rows = lax.broadcasted_iota(jnp.int32, v.shape, 0)
    for step in (1, 2, 4, 8):
        v = v + jnp.where(rows >= step, pltpu.roll(v, step, 0), 0.0)
    return v


def kernel(
    n_cell, x_hbm, sp_hbm, cnt_hbm, w_hbm, head_hbm, din_hbm, dout_hbm, cg_hbm,
    red_ref, hg_ref, igf_ref, og_ref, x_ref,
    sp_ref, cnt_ref, w_ref, head_ref, din_ref, dout_ref, cg_ref, cgt_ref,
    h_ref, s_ref, f_ref, dph_ref, dpl_ref,
    wt_ref, wb_ref, v_ref, dv_ref, dh_ref, headt_ref,
    z_ref, sm_ref, et_ref, hacc_ref,
    p_ref, pr_ref, t_ref, tr_ref, q_ref, qs_ref, l_ref, lr_ref, px_ref, dpre_ref, ogs_ref,
    igs_ref, igr_ref, ex_ref, exc_ref, eb_ref, ef_ref, hx_ref, xs_ref,
    g_ref, cr_ref, half_ref, rr_ref,
    x_sem, in_sem, e1_send, e1_recv, t_send, t_recv, e2_send, e2_recv, l_send, l_recv,
    ig_send, ig_recv, ec_send, ec_recv, eb_send, eb_recv, ef_send, ef_recv, ia_send, ia_recv, hx_send, hx_recv,
    c_send, c_recv, r_send, r_recv, a_send, a_recv, s_send, s_recv,
):
    me = lax.axis_index("cell")
    ray = lax.axis_index("rays")
    core = lax.rem(ray, 2)
    spot = ray // 2
    sibling = ray + 1 - 2 * core
    n_groups = sp_ref.shape[1] // GROUP
    n_spot = 8
    owned = GROUP // n_cell
    wide = 8 * GROUP
    my_rows = pl.ds(pl.multiple_of(me * owned, 8), owned)

    def take(g, side):
        part = pl.ds(g * GROUP * SLOTS, GROUP * SLOTS)
        lanes = pl.ds(side * 128, 128)
        return pltpu.make_async_copy(x_hbm.at[part, lanes], x_ref.at[side, part, :], x_sem.at[g, side])

    pairs = (
        (head_hbm, head_ref), (sp_hbm, sp_ref), (cnt_hbm, cnt_ref), (cg_hbm, cg_ref), (dout_hbm, dout_ref),
        (din_hbm, din_ref),
    )
    small = [pltpu.make_async_copy(src, dst, in_sem.at[n]) for n, (src, dst) in enumerate(pairs)]
    weights = [
        pltpu.make_async_copy(w_hbm.at[l], w_ref.at[l], in_sem.at[len(pairs) + l]) for l in range(LAYERS)
    ]
    weights[0].start()
    for g in range(n_groups):
        for side in range(2):
            take(g, side).start()
        if g == 0:
            for c in weights[1:] + small:
                c.start()

    def cell_peer(d):
        return {"cell": lax.rem(me + d, n_cell)}

    def spot_peer(d):
        return {"rays": 2 * lax.rem(spot + d, n_spot) + core}

    def ray_peer(d):
        return {"rays": lax.rem(ray + d, 2 * n_spot)}

    barrier = pltpu.get_barrier_semaphore()

    def greet(d, _):
        pl.semaphore_signal(barrier, inc=1, device_id=cell_peer(d))
        return 0

    def greet_rays(d, _):
        pl.semaphore_signal(barrier, inc=1, device_id=ray_peer(d))
        return 0

    lax.fori_loop(1, n_cell, greet, 0)
    lax.fori_loop(1, 2 * n_spot, greet_rays, 0)

    def remote(src, dst, send, recv, device):
        return pltpu.make_async_remote_copy(
            src_ref=src, dst_ref=dst, send_sem=send, recv_sem=recv, device_id=device
        )

    def each(count, make):
        def body(d, _):
            make(d).start()
            return 0

        lax.fori_loop(1, count, body, 0)

    def e1(g, d):
        to = lax.rem(me + d, n_cell)
        rows = pl.ds(pl.multiple_of(to * owned, 8), owned)
        return remote(p_ref.at[g, rows, :], pr_ref.at[g, me], e1_send.at[g], e1_recv.at[g], cell_peer(d))

    def e1_all(g):
        blocks = pr_ref.at[g, pl.ds(0, n_cell - 1)]
        return remote(blocks, blocks, e1_send.at[g], e1_recv.at[g], cell_peer(1))

    def t1(g, d):
        return remote(t_ref.at[g], tr_ref.at[g, me], t_send.at[g], t_recv.at[g], cell_peer(d))

    def t1_all(g):
        blocks = tr_ref.at[g, pl.ds(0, n_cell - 1)]
        return remote(blocks, blocks, t_send.at[g], t_recv.at[g], cell_peer(1))

    def e2(g, d):
        return remote(qs_ref.at[g], q_ref.at[g, my_rows, :], e2_send.at[g], e2_recv.at[g], cell_peer(d))

    def e2_all(g):
        blocks = q_ref.at[g, pl.ds(0, GROUP - owned), :]
        return remote(blocks, blocks, e2_send.at[g], e2_recv.at[g], cell_peer(1))

    def l2(g, d):
        return remote(l_ref.at[g], lr_ref.at[g, me], l_send.at[g], l_recv.at[g], cell_peer(d))

    def l2_all(g):
        blocks = lr_ref.at[g, pl.ds(0, n_cell - 1)]
        return remote(blocks, blocks, l_send.at[g], l_recv.at[g], cell_peer(1))

    def igc(d):
        to = lax.rem(me + d, n_cell)
        return remote(igs_ref.at[to], igr_ref.at[me], ig_send.at[0], ig_recv.at[0], cell_peer(d))

    def igc_all():
        blocks = igr_ref.at[pl.ds(0, n_cell - 1)]
        return remote(blocks, blocks, ig_send.at[0], ig_recv.at[0], cell_peer(1))

    ex_mine = pl.ds(pl.multiple_of(core * 24, 8), 24)
    ex_other = pl.ds(pl.multiple_of((1 - core) * 24, 8), 24)

    def ecc():
        return remote(ex_ref.at[ex_other, :], exc_ref, ec_send.at[0], ec_recv.at[0], {"rays": sibling})

    def ebc(d):
        return remote(eb_ref.at[spot], eb_ref.at[spot], eb_send.at[0], eb_recv.at[0], spot_peer(d))

    def ebc_all():
        blocks = eb_ref.at[pl.ds(0, n_spot - 1)]
        return remote(blocks, blocks, eb_send.at[0], eb_recv.at[0], spot_peer(1))

    def efc():
        return remote(ef_ref.at[ex_mine, :], ef_ref.at[ex_mine, :], ef_send.at[0], ef_recv.at[0], {"rays": sibling})

    def iac(d):
        return remote(ef_ref.at[pl.ds(0, 32), :], igf_ref.at[me], ia_send.at[0], ia_recv.at[0], cell_peer(d))

    def iac_all():
        blocks = igf_ref.at[pl.ds(0, n_cell - 1)]
        return remote(blocks, blocks, ia_send.at[0], ia_recv.at[0], cell_peer(1))

    def hx(d):
        return remote(hx_ref.at[ray], hx_ref.at[ray], hx_send.at[0], hx_recv.at[0], ray_peer(d))

    def hx_all():
        blocks = hx_ref.at[pl.ds(0, 2 * n_spot - 1)]
        return remote(blocks, blocks, hx_send.at[0], hx_recv.at[0], ray_peer(1))

    def cc(l):
        other = pl.ds(pl.multiple_of((1 - core) * 128, 128), 128)
        return remote(g_ref.at[l, other, :], cr_ref.at[l], c_send.at[l], c_recv.at[l], {"rays": sibling})

    def rc(l, d):
        to = lax.rem(spot + d, n_spot)
        rows = pl.ds(pl.multiple_of(to * 16, 16), 16)
        return remote(half_ref.at[l, rows, :], rr_ref.at[l, spot], r_send.at[l], r_recv.at[l], spot_peer(d))

    def rc_all(l):
        blocks = rr_ref.at[l, pl.ds(0, n_spot - 1)]
        return remote(blocks, blocks, r_send.at[l], r_recv.at[l], spot_peer(1))

    red_half = pl.ds(pl.multiple_of(core * 128, 128), 128)
    red_block = pl.ds(pl.multiple_of(core * 128 + spot * 16, 16), 16)

    def ac(l, d):
        return remote(red_ref.at[l, red_block, :], red_ref.at[l, red_block, :], a_send.at[l], a_recv.at[l], spot_peer(d))

    def ac_all(l):
        blocks = red_ref.at[l, pl.ds(0, 112), :]
        return remote(blocks, blocks, a_send.at[l], a_recv.at[l], spot_peer(1))

    def sc(l):
        return remote(red_ref.at[l, red_half, :], red_ref.at[l, red_half, :], s_send.at[l], s_recv.at[l], {"rays": sibling})

    def forward_weights(l):
        weights[l].wait()
        thi, tlo = split(w_ref[l].T)
        wt_ref[l] = left3(thi, tlo, 1)
        if l == 0:
            v_ref[...] = left3(thi, tlo, 0)

    def backward_weights():
        for l in range(1, LAYERS):
            wb_ref[l] = left3(*split(w_ref[l]), 1)

    def ray_inputs():
        for c in small:
            c.wait()
        headt_ref[...] = jnp.broadcast_to(head_ref[...], (GROUP, D)).T
        slot = lax.broadcasted_iota(jnp.int32, (SLOTS, GROUP), 0)
        for g in range(n_groups):
            rays = slice(g * GROUP, (g + 1) * GROUP)
            sm_ref[g, 0] = jnp.where(slot < cnt_ref[:, rays], sp_ref[:, rays], 0.0)

    def decoder_inputs():
        hi, lo = split(din_ref[...])
        dv_ref[...] = left3(hi, lo, 0)
        dh_ref[...] = left3(hi, lo, 1)
        ogs_ref[...] = jnp.zeros_like(ogs_ref)
        for g in range(n_groups):
            et_ref[...] = jnp.zeros_like(et_ref)
            et_ref[0:COLORS, :] = cg_ref[:, g * GROUP:(g + 1) * GROUP]
            cgt_ref[g] = et_ref[...].T

    def x_rows(g, s):
        return pl.ds(g * GROUP * SLOTS + s, GROUP, stride=SLOTS)

    def x_load(g, s):
        return jnp.concatenate([x_ref[side, x_rows(g, s), :] for side in range(2)], axis=1)

    def forward(g, half):
        chunk = 2 * g + half
        hidden = [None] * 4
        for q in range(4):
            slabs = [x_load(g, 8 * half + 2 * q + t) for t in range(2)]
            hidden[q] = right3(*split(jnp.concatenate(slabs, axis=0)), 1)
        for l in range(LAYERS):
            for q in range(4):
                columns = pl.ds(q * 2 * GROUP, 2 * GROUP)
                pre = mm(wt_ref[l], hidden[q], NT if l == 0 else NN)
                act, slope = silu_and_slope(pre)
                s_ref[l, chunk, :, columns] = slope
                if l < LAYERS - 1:
                    hi, lo = split(act)
                    h_ref[l, 0, chunk, :, columns] = hi
                    h_ref[l, 1, chunk, :, columns] = lo
                    hidden[q] = right3(hi, lo, 0)
                else:
                    f_ref[chunk, :, columns] = act
                    for t in range(2):
                        z = jnp.sum(act[:, t * GROUP:(t + 1) * GROUP] * headt_ref[...], axis=0, keepdims=True)
                        z_ref[g, pl.ds(8 * half + 2 * q + t, 1), :] = z

    def slot_of(ref, g, s):
        return ref[2 * g + s // 8, :, (s % 8) * GROUP:(s % 8 + 1) * GROUP]

    def rays_forward(g):
        z = z_ref[g]
        tau = softplus(z) * sm_ref[g, 0]
        incl = cumulative(tau)
        excl = incl - tau
        opaque = one_minus_exp(tau)
        sm_ref[g, 1] = tau
        sm_ref[g, 2] = excl
        sm_ref[g, 3] = opaque
        sm_ref[g, 4] = sm_ref[g, 0] * jax.nn.sigmoid(z)
        total = jnp.broadcast_to(incl[SLOTS - 1:SLOTS, :], (8, GROUP))
        t_ref[g] = total
        tr_ref[g, me] = total
        each(n_cell, functools.partial(t1, g))
        local = jnp.exp(-excl) * opaque
        acc = slot_of(f_ref, g, 0) * local[0:1, :]
        for s in range(1, SLOTS):
            acc = acc + slot_of(f_ref, g, s) * local[s:s + 1, :]
        p_ref[g] = acc.T
        each(n_cell, functools.partial(e1, g))
        pr_ref[g, me] = p_ref[g, my_rows, :]

    def decode(g):
        t1_all(g).wait_recv()
        e1_all(g).wait_recv()
        offset = jnp.zeros((1, GROUP), F32)
        own = jnp.zeros((1, GROUP), F32)
        rows = []
        for j in range(n_cell):
            rows.append(jnp.exp(-offset))
            own = jnp.where(me == j, offset, own)
            offset = offset + tr_ref[g, j][0:1, :]
        sm_ref[g, 5] = jnp.broadcast_to(own, (SLOTS, GROUP))
        et_ref[...] = jnp.concatenate(rows + [jnp.zeros((GROUP - n_cell, GROUP), F32)], axis=0).T
        et = et_ref[my_rows, :]
        parts = [pr_ref[g, j] * et[:, j:j + 1] for j in range(n_cell)]
        pixel = parts[0]
        for j in range(1, n_cell):
            pixel = pixel + parts[j]
        px_ref[g] = pixel
        pre = mm(right3(*split(pixel), 1), dv_ref[...], NN)
        colors = cgt_ref[g, my_rows, :]
        act, slope = silu_and_slope(pre)
        reach = colors[:, 0:1] * dout_ref[0:1, :]
        for c in range(1, COLORS):
            reach = reach + colors[:, c:c + 1] * dout_ref[c:c + 1, :]
        dpre = reach * slope
        dpre_ref[g] = dpre
        for c in range(COLORS):
            ogs_ref[g, c:c + 1, :] = jnp.sum(act * colors[:, c:c + 1], axis=0, keepdims=True)
        grad = mm(right3(*split(dpre), 1), dh_ref[...], NT)
        qs_ref[g] = grad
        each(n_cell, functools.partial(e2, g))
        q_ref[g, my_rows, :] = grad
        lanes = lax.broadcasted_iota(jnp.int32, (owned, GROUP), 1)
        later = jnp.zeros((owned, GROUP), F32)
        for j in range(1, n_cell):
            value = jnp.sum(parts[j] * grad, axis=1, keepdims=True)
            later = later + jnp.where(lanes < j, value, 0.0)
        et_ref[...] = jnp.zeros_like(et_ref)
        et_ref[my_rows, :] = later
        tile = et_ref[...].T[0:8, :]
        l_ref[g] = tile
        lr_ref[g, me] = tile
        each(n_cell, functools.partial(l2, g))

    def decoder_grads():
        px = right3(*split(px_ref[...].reshape(n_groups * owned, D)), 0)
        dp = left3(*split(dpre_ref[...].reshape(n_groups * owned, D)), 0)
        grad = mm(px, dp, TN)
        colors = ogs_ref[0]
        for g in range(1, n_groups):
            colors = colors + ogs_ref[g]
        for j in range(n_cell):
            igs_ref[j, 0:32, :] = grad[32 * j:32 * j + 32, :]
            igs_ref[j, 32:40, :] = colors
        each(n_cell, igc)
        igr_ref[me] = igs_ref[me]

    def rays_backward(g):
        e2_all(g).wait_recv()
        gradt = q_ref[g].T
        et_ref[...] = jnp.zeros_like(et_ref)
        for s in range(SLOTS):
            et_ref[s:s + 1, :] = jnp.sum(slot_of(f_ref, g, s) * gradt, axis=0, keepdims=True)
        l2_all(g).wait_recv()
        latert = lr_ref[g, 0]
        for j in range(1, n_cell):
            latert = latert + lr_ref[g, j]
        picked = lax.broadcasted_iota(jnp.int32, (8, GROUP), 0) == me
        later = jnp.sum(jnp.where(picked, latert, 0.0), axis=0, keepdims=True)
        c = et_ref[0:SLOTS, :]
        tau = sm_ref[g, 1]
        trans = jnp.exp(-(sm_ref[g, 5] + sm_ref[g, 2]))
        weight = trans * sm_ref[g, 3]
        incl = cumulative(weight * c)
        after = later + incl[SLOTS - 1:SLOTS, :] - incl
        dz = sm_ref[g, 4] * (trans * jnp.exp(-tau) * c - after)
        sm_ref[g, 6] = weight
        sm_ref[g, 7] = dz
        q_ref[g, :, 0:GROUP] = gradt[0:GROUP, :]
        q_ref[g, :, GROUP:2 * GROUP] = gradt[GROUP:D, :]

    def head_step(chunk, l):
        g, half = chunk // 2, lax.rem(chunk, 2)
        for part in range(4):
            rows = pl.ds(part * 64, 64)
            gradt = q_ref[g, pl.ds((part % 2) * 64, 64), (part // 2) * GROUP:(part // 2 + 1) * GROUP]
            head = headt_ref[rows, :]
            acc = hacc_ref[rows, :]
            for q in range(8):
                row = pl.ds(8 * half + q, 1)
                weight, dz = sm_ref[g, 6, row, :], sm_ref[g, 7, row, :]
                columns = pl.ds(q * GROUP, GROUP)
                acc = acc + f_ref[chunk, rows, columns] * dz
                back = gradt * weight + head * dz
                hi, lo = split(back * s_ref[LAYERS - 1, chunk, rows, columns])
                dph_ref[chunk, rows, columns] = hi
                dpl_ref[chunk, rows, columns] = lo
            hacc_ref[rows, :] = acc

    def layer_step(chunk, l):
        hi, lo = dph_ref[chunk], dpl_ref[chunk]
        source = right3(h_ref[l - 1, 0, chunk], h_ref[l - 1, 1, chunk], 1)
        g_ref[l] += mm(source, left3(hi, lo, 1), NT)
        for q in range(4):
            columns = slice(q * 2 * GROUP, (q + 1) * 2 * GROUP)
            back = mm(wb_ref[l], right3(hi[:, columns], lo[:, columns], 0), NN)
            nhi, nlo = split(back * s_ref[l - 1, chunk, :, columns])
            dph_ref[chunk, :, columns] = nhi
            dpl_ref[chunk, :, columns] = nlo

    def x_split(chunk):
        g, half = chunk // 2, lax.rem(chunk, 2)
        for q in range(8):
            hi, lo = split(x_load(g, 8 * half + q))
            xs_ref[0, chunk, q * GROUP:(q + 1) * GROUP, :] = hi
            xs_ref[1, chunk, q * GROUP:(q + 1) * GROUP, :] = lo

    def first_grad(chunk):
        rows = right3(xs_ref[0, chunk], xs_ref[1, chunk], 0)
        g_ref[0] += mm(left3(dph_ref[chunk], dpl_ref[chunk], 1), rows, NN)

    def first_back(chunk):
        g, half = chunk // 2, lax.rem(chunk, 2)
        for q in range(4):
            columns = slice(q * 2 * GROUP, (q + 1) * 2 * GROUP)
            back = mm(right3(dph_ref[chunk, :, columns], dpl_ref[chunk, :, columns], 0), v_ref[...], TN)
            for t in range(2):
                for side in range(2):
                    x_ref[side, x_rows(g, 8 * half + 2 * q + t), :] = back[
                        t * GROUP:(t + 1) * GROUP, side * 128:(side + 1) * 128
                    ]

    def sum_a(l):
        cc(l).start()

    def sum_b(l):
        cc(l).wait_recv()
        half_ref[l] = g_ref[l, red_half, :] + cr_ref[l]
        each(n_spot, functools.partial(rc, l))
        rr_ref[l, spot] = half_ref[l, pl.ds(pl.multiple_of(spot * 16, 16), 16), :]

    def sum_c(l):
        rc_all(l).wait_recv()
        total = rr_ref[l, 0]
        for j in range(1, n_spot):
            total = total + rr_ref[l, j]
        red_ref[l, red_block, :] = total
        each(n_spot, functools.partial(ac, l))

    def sum_d(l):
        ac_all(l).wait_recv()
        sc(l).start()

    def sum_e(l):
        sc(l).wait_recv()

    def extra_a():
        igc_all().wait_recv()
        total = igr_ref[0]
        for j in range(1, n_cell):
            total = total + igr_ref[j]
        ex_ref[0:40, :] = total
        ecc().start()

    def extra_b():
        ecc().wait_recv()
        eb_ref[spot] = ex_ref[ex_mine, :] + exc_ref[...]
        each(n_spot, ebc)

    def extra_c():
        ebc_all().wait_recv()
        total = eb_ref[0]
        for j in range(1, n_spot):
            total = total + eb_ref[j]
        ef_ref[ex_mine, :] = total
        efc().start()

    def extra_d():
        efc().wait_recv()
        each(n_cell, iac)
        igf_ref[me] = ef_ref[0:32, :]

    def extra_e():
        iac_all().wait_recv()
        og_ref[...] = ef_ref[32:32 + COLORS, :]

    def head_a():
        hx_ref[ray] = jnp.broadcast_to(jnp.sum(hacc_ref[...].T, axis=0, keepdims=True), (8, D))
        each(2 * n_spot, hx)

    def head_b():
        hx_all().wait_recv()
        total = hx_ref[0]
        for j in range(1, 2 * n_spot):
            total = total + hx_ref[j]
        hg_ref[...] = total[0:1, :]

    def wait_x(g):
        for side in range(2):
            take(g, side).wait()

    def forward_loop(g):
        def body(half, _):
            forward(g, half)
            return 0

        lax.fori_loop(0, 2, body, 0)

    def rest(first_chunk, step, between=None):
        def body(chunk, _):
            step(chunk)
            if between is not None:
                pl.when(chunk == first_chunk)(between)
            return 0

        lax.fori_loop(first_chunk, first_chunk + 2, body, 0)

    def top(chunk):
        head_step(chunk, LAYERS - 1)
        layer_step(chunk, LAYERS - 1)

    middle = [functools.partial(layer_step, l=l) for l in range(LAYERS)]
    forward_weights(0)
    ray_inputs()
    for l in range(1, LAYERS):
        forward_weights(l)
    wait_x(0)
    forward_loop(0)
    pl.semaphore_wait(barrier, n_cell - 1 + 2 * n_spot - 1)
    rays_forward(0)
    wait_x(1)
    forward_loop(1)
    rays_forward(1)
    decoder_inputs()
    decode(0)
    backward_weights()
    g_ref[...] = jnp.zeros_like(g_ref)
    hacc_ref[...] = jnp.zeros_like(hacc_ref)
    ex_ref[40:48, :] = jnp.zeros((8, D), F32)
    rest(0, x_split)
    rest(2, x_split)
    decode(1)
    decoder_grads()
    rays_backward(0)
    rest(0, top)
    rest(0, middle[2])
    rays_backward(1)
    extra_a()
    rest(2, top, extra_b)
    sum_a(3)
    head_a()

    rest(2, middle[2], lambda: sum_b(3))
    sum_a(2)
    rest(0, middle[1], lambda: sum_b(2))
    rest(2, middle[1], extra_c)
    sum_a(1)
    extra_d()

    def sums_b1_c3():
        sum_b(1)
        sum_c(3)

    rest(0, first_grad, sums_b1_c3)
    rest(2, first_grad)
    g_ref[0] = g_ref[0].T
    sum_a(0)
    rest(0, first_back, lambda: sum_b(0))
    sum_c(2)
    rest(2, first_back)
    sum_c(1)
    sum_d(3)
    head_b()
    sum_c(0)
    sum_d(2)
    extra_e()
    sum_d(1)
    sum_e(3)
    sum_e(2)
    sum_d(0)
    sum_e(1)
    sum_e(0)
    for g in range(n_groups):
        t1_all(g).wait_send()
        e1_all(g).wait_send()
        e2_all(g).wait_send()
        l2_all(g).wait_send()
    igc_all().wait_send()
    ecc().wait_send()
    ebc_all().wait_send()
    efc().wait_send()
    iac_all().wait_send()
    hx_all().wait_send()
    for l in range(LAYERS):
        cc(l).wait_send()
        rc_all(l).wait_send()
        ac_all(l).wait_send()
        sc(l).wait_send()


def hand_over(lg_ref, hg_ref, ig_ref, og_ref, sg_ref, lg_hbm, hg_hbm, ig_hbm, og_hbm, sg_hbm, sems):
    copies = [
        pltpu.make_async_copy(src, dst, sems.at[n])
        for n, (src, dst) in enumerate(
            ((lg_ref, lg_hbm), (hg_ref, hg_hbm), (ig_ref, ig_hbm), (og_ref, og_hbm))
        )
    ]
    pieces = 4
    rows = sg_hbm.shape[0] // pieces
    for n in range(2 * pieces):
        part, lanes = pl.ds(n // 2 * rows, rows), pl.ds(n % 2 * 128, 128)
        copies.append(pltpu.make_async_copy(sg_ref.at[n % 2, part, :], sg_hbm.at[part, lanes], sems.at[4 + n]))
    for c in copies[::-1]:
        c.start()
    for c in copies:
        c.wait()


def local(n_cell, encodings, spacing, counts, cell_weights, density_head, decoder_in, decoder_out, color_grad):
    rays, slots, width = encodings.shape
    rows = rays * slots
    groups, chunks, wide = rays // GROUP, rows // (8 * GROUP), 8 * GROUP
    owned = GROUP // n_cell
    vmem = pl.BlockSpec(memory_space=pltpu.VMEM)
    anywhere = pl.BlockSpec(memory_space=pl.ANY)
    dma = pltpu.SemaphoreType.DMA
    V = pltpu.VMEM
    scratch = [
        V((slots, rays), F32),
        V((1, rays), jnp.int32),
        V((LAYERS, D, D), F32),
        V((1, D), F32),
        V((D, D), F32),
        V((COLORS, D), F32),
        V((COLORS, rays), F32),
        V((groups, GROUP, GROUP), F32),
        V((LAYERS - 1, 2, chunks, D, wide), BF16),
        V((LAYERS, chunks, D, wide), F32),
        V((chunks, D, wide), F32),
        V((chunks, D, wide), BF16),
        V((chunks, D, wide), BF16),
        V((LAYERS, D, 3 * D), BF16),
        V((LAYERS, D, 3 * D), BF16),
        V((3 * D, D), BF16),
        V((3 * D, D), BF16),
        V((D, 3 * D), BF16),
        V((D, GROUP), F32),
        V((groups, SLOTS, GROUP), F32),
        V((groups, 8, SLOTS, GROUP), F32),
        V((GROUP, GROUP), F32),
        V((D, GROUP), F32),
        V((groups, GROUP, D), F32),
        V((groups, n_cell, owned, D), F32),
        V((groups, 8, GROUP), F32),
        V((groups, n_cell, 8, GROUP), F32),
        V((groups, GROUP, D), F32),
        V((groups, owned, D), F32),
        V((groups, 8, GROUP), F32),
        V((groups, n_cell, 8, GROUP), F32),
        V((groups, owned, D), F32),
        V((groups, owned, D), F32),
        V((groups, 8, D), F32),
        V((n_cell, 40, D), F32),
        V((n_cell, 40, D), F32),
        V((48, D), F32),
        V((24, D), F32),
        V((8, 24, D), F32),
        V((48, D), F32),
        V((16, 8, D), F32),
        V((2, chunks, wide, D), BF16),
        V((LAYERS, D, D), F32),
        V((LAYERS, 128, D), F32),
        V((LAYERS, 128, D), F32),
        V((LAYERS, 8, 16, D), F32),
        dma((groups, 2)), dma((6 + LAYERS,)),
        dma((groups,)), dma((groups,)),
        dma((groups,)), dma((groups,)),
        dma((groups,)), dma((groups,)),
        dma((groups,)), dma((groups,)),
        dma((1,)), dma((1,)),
        dma((1,)), dma((1,)),
        dma((1,)), dma((1,)),
        dma((1,)), dma((1,)),
        dma((1,)), dma((1,)),
        dma((1,)), dma((1,)),
        dma((LAYERS,)), dma((LAYERS,)),
        dma((LAYERS,)), dma((LAYERS,)),
        dma((LAYERS,)), dma((LAYERS,)),
        dma((LAYERS,)), dma((LAYERS,)),
    ]
    outs = [V((LAYERS, D, D), F32), V((1, D), F32), V((n_cell, 32, D), F32), V((COLORS, D), F32), V((2, rows, 128), F32)]
    parts = pl.pallas_call(
        functools.partial(kernel, n_cell),
        out_shape=outs,
        in_specs=[anywhere] * 8,
        out_specs=[vmem] * 5,
        scratch_shapes=scratch,
        compiler_params=pltpu.CompilerParams(
            collective_id=0, has_side_effects=True, vmem_limit_bytes=56 << 20
        ),
    )(
        encodings.reshape(rows, width), spacing.T, counts.T, cell_weights[0], density_head,
        decoder_in, decoder_out.T, color_grad.T,
    )
    layer, head, din, dout, sample = pl.pallas_call(
        hand_over,
        out_shape=[
            jax.ShapeDtypeStruct((LAYERS, D, D), F32),
            jax.ShapeDtypeStruct((1, D), F32),
            jax.ShapeDtypeStruct((n_cell, 32, D), F32),
            jax.ShapeDtypeStruct((COLORS, D), F32),
            jax.ShapeDtypeStruct((rows, D), F32),
        ],
        in_specs=[vmem] * 5,
        out_specs=[anywhere] * 5,
        scratch_shapes=[dma((12,))],
        compiler_params=pltpu.CompilerParams(vmem_limit_bytes=1 << 20),
    )(*(pltpu.with_memory_space_constraint(part, pltpu.VMEM) for part in parts))
    return layer[None], head, din.reshape(D, D), dout.T, sample.reshape(rays, slots, width)


def solution(mesh):
    return jax.shard_map(
        functools.partial(local, mesh.shape["cell"]),
        mesh=mesh,
        in_specs=(
            P("rays", "cell", None), P("rays", "cell"), P("rays", "cell"), P("cell", None, None, None),
            P("cell", None), P(None, None), P(None, None), P("rays", None),
        ),
        out_specs=(
            P("cell", None, None, None), P("cell", None), P(None, None), P(None, None), P("rays", "cell", None),
        ),
        check_vma=False,
    )
```
